256 devices in a mesh: src: 8 (over x, z_lo), tgt: 4 (over z_hi), feat: 8 (over y, core).
Axes of the slice: x: 4, y: 4, z: 8 (z_hi: 4, z_lo: 2; z = z_hi * 2 + z_lo), core: 2. Of those that a mesh axis runs over, the one named last changes fastest.
Arguments:
- errors: bfloat16 [8, 1024, 2048], P('tgt', 'feat', 'src'), may hold values from -0.796875 to 0.796875
- saved_codes: bfloat16 [8, 1024, 4096], P('src', None, 'feat'), may hold values from 0 to 2
- active_mask: int32 [8, 1024, 4096], P('src', 'tgt', 'feat'), may hold values 0 or 1
- decoder: bfloat16 [8, 8, 4096, 2048], P('src', 'tgt', 'feat'), may hold values from -0.09375 to 0.09375
Outputs:
- code_grads: bfloat16 [8, 1024, 4096], P('src', 'tgt', 'feat')
- decoder_grads: bfloat16 [8, 8, 4096, 2048], P('src', 'tgt', 'feat')
The draws below stay inside these ranges and needn't reach their ends.
All inputs are finite; a program needn't handle non-finite values. No bound on the sum of `active_mask` on one device may be relied on, other than what follows from the above.
Results may differ from the reference program's by a relative error of at most 0.001.
Values may be sent and summed in bfloat16 or wider, within the bound.
A program may use at most 128 MiB of HBM per device.

```python
import jax
import jax.numpy as jnp

D = 2048
LAYERS = 8
TOKENS = 1024
FEATS = 4096


def plant(array, own_key, least, high):
    dims = array.shape
    spot = [jax.random.randint(jax.random.fold_in(own_key, axis), (), 0, dims[axis]) for axis in range(len(dims))]
    array = array.at[tuple(spot)].set(least)
    longest = dims.index(max(dims))
    spot[longest] = (spot[longest] + 1) % dims[longest]
    return array.at[tuple(spot)].set(high)


def block_scale(own_key, extent, split, least, high):
    loudness, own = 1.0, jax.random.fold_in(own_key, 6)
    for position, shards_of in split:
        steps = jnp.exp(jax.random.uniform(jax.random.fold_in(own, position), (shards_of,), jnp.float32, least / len(split), high / len(split)))
        loudness = loudness * jnp.repeat(steps, extent[position] // shards_of).reshape([-1 if axis == position else 1 for axis in range(len(extent))])
    return loudness


def bell_draw(key, extent, spread, most, pieces=(), dtype=jnp.bfloat16):
    array = spread * jax.random.normal(key, extent, jnp.float32)
    if pieces:
        array = array * block_scale(key, extent, pieces, -0.22, 0.18)
    return jnp.clip(array, -most, most).astype(dtype)


def setup_inputs(seed: int = 0) -> dict:
    keys = jax.random.split(jax.random.key(seed), 5)
    return {
        "errors": bell_draw(keys[0], (LAYERS, TOKENS, D), 0.1, 0.796875, ((0, 4), (1, 8), (2, 8))),
        "saved_codes": jnp.clip(2.0 * jax.random.uniform(keys[1], (LAYERS, TOKENS, FEATS), jnp.float32) ** block_scale(keys[1], (LAYERS, TOKENS, FEATS), ((0, 8), (2, 8)), -0.2, 0.2), 0.0, 2.0).astype(jnp.bfloat16),
        "active_mask": plant((jax.random.randint(keys[2], (LAYERS, TOKENS, FEATS), 0, 3) < 1).astype(jnp.int32), jax.random.fold_in(keys[2], 1), 0, 1),
        "decoder": bell_draw(keys[3], (LAYERS, LAYERS, FEATS, D), FEATS ** -0.5, 0.09375, ((0, 8), (1, 4), (2, 8))),
    }


def reference(errors, saved_codes, active_mask, decoder):
    grad_rows = []
    code_rows = []
    for src_layer in range(LAYERS):
        tile_row = []
        summed = jnp.zeros((TOKENS, FEATS), jnp.float32)
        for tgt_layer in range(LAYERS):
            if tgt_layer >= src_layer:
                tile = jnp.dot(saved_codes[src_layer].T, errors[tgt_layer], preferred_element_type=jnp.float32)
                tile_row.append(tile.astype(jnp.bfloat16))
                summed = summed + jnp.dot(errors[tgt_layer], decoder[src_layer, tgt_layer].T, preferred_element_type=jnp.float32)
            else:
                tile_row.append(jnp.zeros((FEATS, D), jnp.bfloat16))
        grad_rows.append(jnp.stack(tile_row))
        code_rows.append((summed * active_mask[src_layer].astype(jnp.float32)).astype(jnp.bfloat16))
    return jnp.stack(code_rows), jnp.stack(grad_rows)
```

```python
import jax
import jax.numpy as jnp
from jax import lax
from jax.experimental import pallas as pl
from jax.experimental.pallas import tpu as pltpu
from jax.sharding import PartitionSpec as P

MESH = pl.DeviceIdType.MESH

NAMES = (
    ["Z"]
    + [a + b for a in "XY" for b in "ABCDEF"]
    + [a + b + str(i) for a in "PQ" for b in "fbo" for i in range(4)]
    + ["D" + str(layer) + str(k) for layer in range(2) for k in range(4)]
    + ["R" + str(i) for i in range(6)]
)
IDS = {name: i for i, name in enumerate(NAMES)}


def kernel(err, codes, mask, dec_hbm, cg, dw, E, codes_v, codes_t, dec, mask_v, part, rbuf, local, ssem, rsem):
    s, t, f = lax.axis_index("src"), lax.axis_index("tgt"), lax.axis_index("feat")
    x, zl = s // 2, s % 2
    y, c = f // 2, f % 2
    step = 1 - 2 * zl
    xf, xb, xo = (x + step + 4) % 4, (x - step + 4) % 4, (x + 2) % 4
    yf, yb, yo = (y + step + 4) % 4, (y - step + 4) % 4, (y + 2) % 4
    X_F, X_B = {"src": xf * 2 + zl}, {"src": xb * 2 + zl}
    Y_F, Y_B = {"feat": yf * 2 + c}, {"feat": yb * 2 + c}
    Z_P, C_P = {"src": x * 2 + 1 - zl}, {"feat": y * 2 + 1 - c}
    T_UP, T_DN = {"tgt": (t + 1) % 4}, {"tgt": (t + 3) % 4}

    def rows(yy, cc):
        return pl.ds(pl.multiple_of((2 * yy + cc) * 128, 128), 128)

    def item(layer, xx, z, yy):
        return E.at[layer, rows(yy, c), pl.ds(pl.multiple_of((2 * xx + z) * 256, 256), 256)]

    def pair(layer, xx, yy):
        return E.at[layer, rows(yy, c), pl.ds(pl.multiple_of(xx * 512, 512), 512)]

    def line(layer, yy, cc):
        return E.at[layer, rows(yy, cc), :]

    sent = []

    def copy(name, src, dst, dev):
        i = IDS[name]
        return pltpu.make_async_remote_copy(
            src_ref=src, dst_ref=dst, send_sem=ssem.at[i], recv_sem=rsem.at[i],
            device_id=dev, device_id_type=MESH,
        )

    def send(name, src, dev, dst=None):
        d = copy(name, src, src if dst is None else dst, dev)
        d.start()
        sent.append(d)

    def got(name, ref):
        copy(name, ref, ref, C_P).wait_recv()

    own_cols = pl.ds(pl.multiple_of(s * 256, 256), 256)
    own = E.at[:, rows(y, c), own_cols]
    load_err = pltpu.make_async_copy(err, own, local.at[0])
    load_codes = pltpu.make_async_copy(codes.at[0], codes_v, local.at[1])
    load_dec = pltpu.make_async_copy(dec_hbm.at[0], dec, local.at[2])
    load_mask = pltpu.make_async_copy(mask.at[0], mask_v, local.at[3])
    load_err.start()
    load_codes.start()
    load_dec.start()
    load_mask.start()

    barrier = pltpu.get_barrier_semaphore()
    for dev in (X_F, X_B, Y_F, Y_B, Z_P, C_P, T_UP, T_DN):
        pl.semaphore_signal(barrier, inc=1, device_id=dev, device_id_type=MESH)
    pl.semaphore_wait(barrier, 8)
    load_err.wait()

    send("Z", own, Z_P)
    send("XA", item(0, x, zl, y), X_F)
    send("XB", item(0, x, zl, y), X_B)
    send("YA", item(1, x, zl, y), Y_F)
    send("YB", item(1, x, zl, y), Y_B)

    load_codes.wait()
    for i in range(4):
        codes_t[i * 128 : (i + 1) * 128, :] = codes_v[:, i * 128 : (i + 1) * 128].T

    oz = 1 - zl
    got("Z", E.at[:, rows(y, c), pl.ds(pl.multiple_of((2 * x + oz) * 256, 256), 256)])
    send("XD", item(0, x, oz, y), X_F)
    send("XE", item(0, x, oz, y), X_B)
    send("YD", item(1, x, oz, y), Y_F)
    send("YE", item(1, x, oz, y), Y_B)

    got("XA", item(0, xb, zl, y))
    send("XC", item(0, xb, zl, y), X_F)
    got("YA", item(1, x, zl, yb))
    send("YC", item(1, x, zl, yb), Y_F)
    got("XE", item(0, xf, oz, y))
    send("XF", item(0, xf, oz, y), X_B)
    got("YE", item(1, x, oz, yf))
    send("YF", item(1, x, oz, yf), Y_B)

    ys, xs = (y, yb, yf, yo), (x, xb, xf, xo)

    def send_p(i):
        send("Pf%d" % i, pair(0, xs[i], y), Y_F)
        send("Pb%d" % i, pair(0, xs[i], y), Y_B)

    def send_q(i):
        send("Qf%d" % i, pair(1, x, ys[i]), X_F)
        send("Qb%d" % i, pair(1, x, ys[i]), X_B)

    send_p(0)
    send_q(0)
    got("XD", item(0, xb, oz, y))
    send_p(1)
    got("YD", item(1, x, oz, yb))
    send_q(1)
    got("XB", item(0, xf, zl, y))
    send_p(2)
    got("YB", item(1, x, zl, yf))
    send_q(2)
    got("XC", item(0, xo, zl, y))
    got("XF", item(0, xo, oz, y))
    send_p(3)
    send("D00", line(0, y, c), C_P)
    got("YC", item(1, x, zl, yo))
    got("YF", item(1, x, oz, yo))
    send_q(3)

    live0, live1 = 2 * t >= s, 2 * t + 1 >= s

    def code_part(layer, k):
        block = pl.ds(pl.multiple_of(ys[k] * 256, 256), 256)
        for n in range(2):
            cols = slice(n * 256, (n + 1) * 256)

            def product():
                return lax.dot_general(
                    E[layer, block, :], dec[layer, cols, :], (((1,), (1,)), ((), ())),
                    preferred_element_type=jnp.float32,
                )

            if layer == 0:

                @pl.when(live0)
                def _():
                    part[k, :, cols] = product()

                @pl.when(jnp.logical_not(live0))
                def _():
                    part[k, :, cols] = jnp.zeros((256, 256), jnp.float32)
            else:

                @pl.when(live1)
                def _():
                    part[k, :, cols] += product()

    lo, hi = slice(0, 128), slice(128, 256)

    def reduce_start(k):
        d = (t - ys[k] + 4) % 4

        @pl.when(d == 2)
        def _():
            copy("R0", part.at[k, lo], rbuf.at[0], T_DN).start()
            copy("R1", part.at[k, hi], rbuf.at[1], T_UP).start()

        @pl.when(d == 1)
        def _():
            copy("R2", part.at[k, hi], rbuf.at[2], T_DN).start()

        @pl.when(d == 3)
        def _():
            copy("R4", part.at[k, lo], rbuf.at[4], T_UP).start()

    def reduce_next(k):
        d = (t - ys[k] + 4) % 4

        @pl.when(d == 1)
        def _():
            got("R0", rbuf.at[0])
            part[k, lo] += rbuf[0]
            copy("R3", part.at[k, lo], rbuf.at[3], T_DN).start()

        @pl.when(d == 3)
        def _():
            got("R1", rbuf.at[1])
            part[k, hi] += rbuf[1]
            copy("R5", part.at[k, hi], rbuf.at[5], T_UP).start()

    def relay(i):
        if i < 2:
            got("Pf%d" % i, pair(0, xs[i], yb))
            send("Po%d" % i, pair(0, xs[i], yb), Y_F)
            got("Qf%d" % i, pair(1, xb, ys[i]))
            send("Qo%d" % i, pair(1, xb, ys[i]), X_F)
        else:
            got("Pb%d" % i, pair(0, xs[i], yf))
            send("Po%d" % i, pair(0, xs[i], yf), Y_B)
            got("Qb%d" % i, pair(1, xf, ys[i]))
            send("Qo%d" % i, pair(1, xf, ys[i]), X_B)

    def rest_q(i):
        if i < 2:
            got("Qb%d" % i, pair(1, xf, ys[i]))
        else:
            got("Qf%d" % i, pair(1, xb, ys[i]))
        got("Qo%d" % i, pair(1, xo, ys[i]))

    relay(0)
    relay(1)
    rest_q(0)
    send("D10", line(1, y, c), C_P)
    load_dec.wait()
    got("D00", line(0, y, 1 - c))
    code_part(0, 0)
    got("D10", line(1, y, 1 - c))
    relay(2)
    code_part(1, 0)
    reduce_start(0)
    relay(3)
    got("Pf2", pair(0, xs[2], yb))
    got("Pf3", pair(0, xs[3], yb))
    send("D01", line(0, yb, c), C_P)
    rest_q(1)
    send("D11", line(1, yb, c), C_P)
    got("Pb0", pair(0, xs[0], yf))
    got("Pb1", pair(0, xs[1], yf))
    send("D02", line(0, yf, c), C_P)
    got("D01", line(0, yb, 1 - c))
    code_part(0, 1)
    rest_q(2)
    send("D12", line(1, yf, c), C_P)
    got("D11", line(1, yb, 1 - c))
    code_part(1, 1)
    reduce_start(1)
    for i in range(4):
        got("Po%d" % i, pair(0, xs[i], yo))
    send("D03", line(0, yo, c), C_P)
    rest_q(3)
    send("D13", line(1, yo, c), C_P)
    got("D02", line(0, yf, 1 - c))
    code_part(0, 2)
    got("D12", line(1, yf, 1 - c))
    code_part(1, 2)
    reduce_start(2)
    reduce_next(0)
    got("D03", line(0, yo, 1 - c))
    code_part(0, 3)
    got("D13", line(1, yo, 1 - c))
    code_part(1, 3)
    reduce_start(3)
    reduce_next(1)

    def tile_grads(layer, live):
        @pl.when(live)
        def _():
            def one(i, carry):
                cols = pl.ds(pl.multiple_of(i * 256, 256), 256)
                dw[0, layer, :, cols] = jnp.dot(
                    codes_t[...], E[layer, :, cols], preferred_element_type=jnp.float32
                ).astype(jnp.bfloat16)
                return carry

            lax.fori_loop(0, 8, one, 0)

        @pl.when(jnp.logical_not(live))
        def _():
            dw[0, layer] = jnp.zeros((512, 2048), jnp.bfloat16)

    tile_grads(0, live0)
    reduce_next(2)
    tile_grads(1, live1)
    reduce_next(3)

    load_mask.wait()
    got("R2", rbuf.at[2])
    got("R4", rbuf.at[4])
    got("R3", rbuf.at[3])
    got("R5", rbuf.at[5])
    for k in range(4):

        @pl.when(ys[k] == t)
        def _():
            low = part[k, lo] + rbuf[4] + rbuf[3]
            high = part[k, hi] + rbuf[2] + rbuf[5]
            cg[0, lo] = (low * mask_v[lo].astype(jnp.float32)).astype(jnp.bfloat16)
            cg[0, hi] = (high * mask_v[hi].astype(jnp.float32)).astype(jnp.bfloat16)

    for d in sent:
        d.wait_send()
    for i in range(6):
        copy("R%d" % i, rbuf.at[i], rbuf.at[i], C_P).wait_send()


def body(errors, saved_codes, active_mask, decoder):
    n = len(NAMES)
    return pl.pallas_call(
        kernel,
        out_shape=(
            jax.ShapeDtypeStruct((1, 256, 512), jnp.bfloat16),
            jax.ShapeDtypeStruct((1, 2, 512, 2048), jnp.bfloat16),
        ),
        in_specs=[pl.BlockSpec(memory_space=pl.ANY)] * 4,
        out_specs=(pl.BlockSpec(memory_space=pltpu.VMEM),) * 2,
        scratch_shapes=[
            pltpu.VMEM((2, 1024, 2048), jnp.bfloat16),
            pltpu.VMEM((1024, 512), jnp.bfloat16),
            pltpu.VMEM((512, 1024), jnp.bfloat16),
            pltpu.VMEM((2, 512, 2048), jnp.bfloat16),
            pltpu.VMEM((256, 512), jnp.int32),
            pltpu.VMEM((4, 256, 512), jnp.float32),
            pltpu.VMEM((6, 128, 512), jnp.float32),
            pltpu.SemaphoreType.DMA((4,)),
            pltpu.SemaphoreType.DMA((n,)),
            pltpu.SemaphoreType.DMA((n,)),
        ],
        compiler_params=pltpu.CompilerParams(
            collective_id=0, has_side_effects=True, vmem_limit_bytes=48 * 1024 * 1024
        ),
    )(errors, saved_codes, active_mask, decoder)


def solution(mesh):
    in_specs = (
        P("tgt", "feat", "src"),
        P("src", None, "feat"),
        P("src", "tgt", "feat"),
        P("src", "tgt", "feat", None),
    )
    out_specs = (P("src", "tgt", "feat"), P("src", "tgt", "feat", None))
    return jax.shard_map(body, mesh=mesh, in_specs=in_specs, out_specs=out_specs, check_vma=False)
```

```python
import jax
import jax.numpy as jnp
from jax import lax
from jax.experimental import pallas as pl
from jax.experimental.pallas import tpu as pltpu
from jax.sharding import PartitionSpec as P

MESH = pl.DeviceIdType.MESH

NAMES = (
    ["Z0", "Z1"]
    + [a + b for a in "XY" for b in ("fA", "bA", "fZ", "bZ", "rfA", "rbA", "rfZ", "rbZ")]
    + [a + b + i for a in "PQ" for b in ("f", "b", "rf", "rb") for i in "AZ123"]
    + ["D" + str(layer) + str(k) for layer in range(2) for k in range(4)]
    + ["R" + str(i) for i in range(6)]
)
IDS = {name: i for i, name in enumerate(NAMES)}


def kernel(err, codes, mask, dec_hbm, cg, dw, E, codes_v, codes_t, dec, mask_v, part, rbuf, local, ssem, rsem):
    s, t, f = lax.axis_index("src"), lax.axis_index("tgt"), lax.axis_index("feat")
    x, zl = s // 2, s % 2
    y, c = f // 2, f % 2
    step = 1 - 2 * zl
    xf, xb, xo = (x + step + 4) % 4, (x - step + 4) % 4, (x + 2) % 4
    yf, yb, yo = (y + step + 4) % 4, (y - step + 4) % 4, (y + 2) % 4
    X_F, X_B = {"src": xf * 2 + zl}, {"src": xb * 2 + zl}
    Y_F, Y_B = {"feat": yf * 2 + c}, {"feat": yb * 2 + c}
    Z_P, C_P = {"src": x * 2 + 1 - zl}, {"feat": y * 2 + 1 - c}
    T_UP, T_DN = {"tgt": (t + 1) % 4}, {"tgt": (t + 3) % 4}

    oz = 1 - zl
    ys, xs = (y, yb, yf, yo), (x, xb, xf, xo)

    def rows(yy, cc, half=None):
        if half is None:
            return pl.ds(pl.multiple_of((2 * yy + cc) * 128, 128), 128)
        return pl.ds(pl.multiple_of((2 * yy + cc) * 128 + half * 64, 64), 64)

    def item(layer, xx, z, yy, half=None):
        return E.at[layer, rows(yy, c, half), pl.ds(pl.multiple_of((2 * xx + z) * 256, 256), 256)]

    def pair(layer, xx, yy, half=None):
        return E.at[layer, rows(yy, c, half), pl.ds(pl.multiple_of(xx * 512, 512), 512)]

    def line(layer, yy, cc):
        return E.at[layer, rows(yy, cc), :]

    sent = []

    def copy(name, src, dst, dev):
        i = IDS[name]
        return pltpu.make_async_remote_copy(
            src_ref=src, dst_ref=dst, send_sem=ssem.at[i], recv_sem=rsem.at[i],
            device_id=dev, device_id_type=MESH,
        )

    def send(name, src, dev, dst=None):
        d = copy(name, src, src if dst is None else dst, dev)
        d.start()
        sent.append(d)

    def got(name, ref):
        copy(name, ref, ref, C_P).wait_recv()

    own_cols = pl.ds(pl.multiple_of(s * 256, 256), 256)
    own = E.at[:, rows(y, c), own_cols]
    load_err = pltpu.make_async_copy(err, own, local.at[0])
    load_codes = pltpu.make_async_copy(codes.at[0], codes_v, local.at[1])
    load_dec = pltpu.make_async_copy(dec_hbm.at[0], dec, local.at[2])
    load_mask = pltpu.make_async_copy(mask.at[0], mask_v, local.at[3])
    load_err.start()
    load_codes.start()
    load_dec.start()
    load_mask.start()

    barrier = pltpu.get_barrier_semaphore()
    for dev in (X_F, X_B, Y_F, Y_B, Z_P, C_P, T_UP, T_DN):
        pl.semaphore_signal(barrier, inc=1, device_id=dev, device_id_type=MESH)
    pl.semaphore_wait(barrier, 8)
    load_err.wait()

    def first(layer, kind, where):
        ax, (fw, bw) = ("X", (X_F, X_B)) if layer == 0 else ("Y", (Y_F, Y_B))
        send(ax + "f" + kind, where, fw)
        send(ax + "b" + kind, where, bw)

    def second(layer, piece, where):
        ax, (fw, bw) = ("P", (Y_F, Y_B)) if layer == 0 else ("Q", (X_F, X_B))
        send(ax + "f" + piece, where, fw)
        send(ax + "b" + piece, where, bw)

    own0, own1 = item(0, x, zl, y), item(1, x, zl, y)
    send("Z0", own0, Z_P)
    send("Z1", own1, Z_P)
    first(0, "A", own0)
    first(1, "A", own1)
    second(1, "A", own1)
    second(0, "A", own0)

    load_codes.wait()
    for i in range(4):
        codes_t[i * 128 : (i + 1) * 128, :] = codes_v[:, i * 128 : (i + 1) * 128].T

    def first_relay(layer, kind):
        z = zl if kind == "A" else oz
        if layer == 0:
            got("Xf" + kind, item(0, xb, z, y))
            send("Xrf" + kind, item(0, xb, z, y, 0), X_F)
            got("Xb" + kind, item(0, xf, z, y))
            send("Xrb" + kind, item(0, xf, z, y, 1), X_B)
        else:
            got("Yf" + kind, item(1, x, z, yb))
            send("Yrf" + kind, item(1, x, z, yb, 0), Y_F)
            got("Yb" + kind, item(1, x, z, yf))
            send("Yrb" + kind, item(1, x, z, yf, 1), Y_B)

    def first_rest(layer):
        for kind, z in (("A", zl), ("Z", oz)):
            if layer == 0:
                got("Xrf" + kind, item(0, xo, z, y, 0))
                got("Xrb" + kind, item(0, xo, z, y, 1))
            else:
                got("Yrf" + kind, item(1, x, z, yo, 0))
                got("Yrb" + kind, item(1, x, z, yo, 1))

    def piece_at(layer, piece, near, half=None):
        if piece in "AZ":
            z = zl if piece == "A" else oz
            return item(0, x, z, near, half) if layer == 0 else item(1, near, z, y, half)
        i = int(piece)
        return pair(0, xs[i], near, half) if layer == 0 else pair(1, near, ys[i], half)

    def second_relay(layer, piece):
        ax, (fw, bw), (nb, nf) = ("P", (Y_F, Y_B), (yb, yf)) if layer == 0 else ("Q", (X_F, X_B), (xb, xf))
        got(ax + "f" + piece, piece_at(layer, piece, nb))
        send(ax + "rf" + piece, piece_at(layer, piece, nb, 0), fw)
        got(ax + "b" + piece, piece_at(layer, piece, nf))
        send(ax + "rb" + piece, piece_at(layer, piece, nf, 1), bw)

    def second_rest(layer, piece):
        ax, far = ("P", yo) if layer == 0 else ("Q", xo)
        got(ax + "rf" + piece, piece_at(layer, piece, far, 0))
        got(ax + "rb" + piece, piece_at(layer, piece, far, 1))

    got("Z0", item(0, x, oz, y))
    first(0, "Z", item(0, x, oz, y))
    second(0, "Z", item(0, x, oz, y))
    first_relay(0, "A")
    first_relay(1, "A")
    got("Z1", item(1, x, oz, y))
    first(1, "Z", item(1, x, oz, y))
    second(1, "Z", item(1, x, oz, y))
    second_relay(1, "A")
    first_relay(0, "Z")
    second(0, "1", pair(0, xb, y))
    second(0, "2", pair(0, xf, y))
    first_relay(1, "Z")
    second_relay(1, "Z")
    second(1, "1", pair(1, x, yb))
    second(1, "2", pair(1, x, yf))
    first_rest(0)
    second(0, "3", pair(0, xo, y))
    send("D00", line(0, y, c), C_P)
    first_rest(1)
    second_rest(1, "A")
    second_rest(1, "Z")
    send("D10", line(1, y, c), C_P)

    live0, live1 = 2 * t >= s, 2 * t + 1 >= s

    def code_part(layer, k):
        block = pl.ds(pl.multiple_of(ys[k] * 256, 256), 256)
        for n in range(2):
            cols = slice(n * 256, (n + 1) * 256)

            def product():
                return lax.dot_general(
                    E[layer, block, :], dec[layer, cols, :], (((1,), (1,)), ((), ())),
                    preferred_element_type=jnp.float32,
                )

            if layer == 0:

                @pl.when(live0)
                def _():
                    part[k, :, cols] = product()

                @pl.when(jnp.logical_not(live0))
                def _():
                    part[k, :, cols] = jnp.zeros((256, 256), jnp.float32)
            else:

                @pl.when(live1)
                def _():
                    part[k, :, cols] += product()

    lo, hi = slice(0, 128), slice(128, 256)

    def reduce_start(k):
        d = (t - ys[k] + 4) % 4

        @pl.when(d == 2)
        def _():
            copy("R0", part.at[k, lo], rbuf.at[0], T_DN).start()
            copy("R1", part.at[k, hi], rbuf.at[1], T_UP).start()

        @pl.when(d == 1)
        def _():
            copy("R2", part.at[k, hi], rbuf.at[2], T_DN).start()

        @pl.when(d == 3)
        def _():
            copy("R4", part.at[k, lo], rbuf.at[4], T_UP).start()

    def reduce_next(k):
        d = (t - ys[k] + 4) % 4

        @pl.when(d == 1)
        def _():
            got("R0", rbuf.at[0])
            part[k, lo] += rbuf[0]
            copy("R3", part.at[k, lo], rbuf.at[3], T_DN).start()

        @pl.when(d == 3)
        def _():
            got("R1", rbuf.at[1])
            part[k, hi] += rbuf[1]
            copy("R5", part.at[k, hi], rbuf.at[5], T_UP).start()

    load_dec.wait()
    got("D00", line(0, y, 1 - c))
    code_part(0, 0)
    second_relay(0, "A")
    second_relay(0, "Z")
    second_relay(1, "1")
    got("D10", line(1, y, 1 - c))
    code_part(1, 0)
    reduce_start(0)
    second_relay(1, "2")
    second(1, "3", pair(1, x, yo))
    second_relay(0, "1")
    second_relay(0, "2")
    second_rest(1, "1")
    send("D11", line(1, yb, c), C_P)
    second_relay(0, "3")
    send("D01", line(0, yb, c), C_P)
    send("D02", line(0, yf, c), C_P)
    second_rest(1, "2")
    send("D12", line(1, yf, c), C_P)
    got("D01", line(0, yb, 1 - c))
    code_part(0, 1)
    second_relay(1, "3")
    got("D11", line(1, yb, 1 - c))
    code_part(1, 1)
    reduce_start(1)
    for piece in "AZ123":
        second_rest(0, piece)
    send("D03", line(0, yo, c), C_P)
    got("D02", line(0, yf, 1 - c))
    code_part(0, 2)
    second_rest(1, "3")
    send("D13", line(1, yo, c), C_P)
    got("D12", line(1, yf, 1 - c))
    code_part(1, 2)
    reduce_start(2)
    reduce_next(0)
    got("D03", line(0, yo, 1 - c))
    code_part(0, 3)
    got("D13", line(1, yo, 1 - c))
    code_part(1, 3)
    reduce_start(3)
    reduce_next(1)

    def tile_grads(layer, live):
        @pl.when(live)
        def _():
            def one(i, carry):
                cols = pl.ds(pl.multiple_of(i * 256, 256), 256)
                dw[0, layer, :, cols] = jnp.dot(
                    codes_t[...], E[layer, :, cols], preferred_element_type=jnp.float32
                ).astype(jnp.bfloat16)
                return carry

            lax.fori_loop(0, 8, one, 0)

        @pl.when(jnp.logical_not(live))
        def _():
            dw[0, layer] = jnp.zeros((512, 2048), jnp.bfloat16)

    tile_grads(0, live0)
    reduce_next(2)
    tile_grads(1, live1)
    reduce_next(3)

    load_mask.wait()
    got("R2", rbuf.at[2])
    got("R4", rbuf.at[4])
    got("R3", rbuf.at[3])
    got("R5", rbuf.at[5])
    for k in range(4):

        @pl.when(ys[k] == t)
        def _():
            low = part[k, lo] + rbuf[4] + rbuf[3]
            high = part[k, hi] + rbuf[2] + rbuf[5]
            cg[0, lo] = (low * mask_v[lo].astype(jnp.float32)).astype(jnp.bfloat16)
            cg[0, hi] = (high * mask_v[hi].astype(jnp.float32)).astype(jnp.bfloat16)

    for d in sent:
        d.wait_send()
    for i in range(6):
        copy("R%d" % i, rbuf.at[i], rbuf.at[i], C_P).wait_send()


def body(errors, saved_codes, active_mask, decoder):
    n = len(NAMES)
    return pl.pallas_call(
        kernel,
        out_shape=(
            jax.ShapeDtypeStruct((1, 256, 512), jnp.bfloat16),
            jax.ShapeDtypeStruct((1, 2, 512, 2048), jnp.bfloat16),
        ),
        in_specs=[pl.BlockSpec(memory_space=pltpu.HBM)] * 4,
        out_specs=(pl.BlockSpec(memory_space=pltpu.VMEM),) * 2,
        scratch_shapes=[
            pltpu.VMEM((2, 1024, 2048), jnp.bfloat16),
            pltpu.VMEM((1024, 512), jnp.bfloat16),
            pltpu.VMEM((512, 1024), jnp.bfloat16),
            pltpu.VMEM((2, 512, 2048), jnp.bfloat16),
            pltpu.VMEM((256, 512), jnp.int32),
            pltpu.VMEM((4, 256, 512), jnp.float32),
            pltpu.VMEM((6, 128, 512), jnp.float32),
            pltpu.SemaphoreType.DMA((4,)),
            pltpu.SemaphoreType.DMA((n,)),
            pltpu.SemaphoreType.DMA((n,)),
        ],
        compiler_params=pltpu.CompilerParams(
            collective_id=0, has_side_effects=True, vmem_limit_bytes=48 * 1024 * 1024
        ),
    )(*(pltpu.with_memory_space_constraint(a, pltpu.HBM) for a in (errors, saved_codes, active_mask, decoder)))


def solution(mesh):
    in_specs = (
        P("tgt", "feat", "src"),
        P("src", None, "feat"),
        P("src", "tgt", "feat"),
        P("src", "tgt", "feat", None),
    )
    out_specs = (P("src", "tgt", "feat"), P("src", "tgt", "feat", None))
    return jax.shard_map(body, mesh=mesh, in_specs=in_specs, out_specs=out_specs, check_vma=False)
```

```python
import jax
import jax.numpy as jnp
from jax import lax
from jax.experimental import pallas as pl
from jax.experimental.pallas import tpu as pltpu
from jax.sharding import PartitionSpec as P

MESH = pl.DeviceIdType.MESH

NAMES = (
    ["Z0", "Z1"]
    + [a + b for a in "XY" for b in ("fA", "bA", "fZ", "bZ", "rfA", "rbA", "rfZ", "rbZ")]
    + [a + b + i for a in "PQ" for b in ("f", "b", "rf", "rb") for i in "AZ123"]
    + ["D" + str(layer) + str(k) for layer in range(2) for k in range(4)]
    + [a + str(i) for a in "RS" for i in range(6)]
)
IDS = {name: i for i, name in enumerate(NAMES)}


def kernel(err, codes, mask, dec_hbm, cg, dw, E, codes_v, codes_t, dec, mask_v, part, qout, sout, qin, sin, local, ssem, rsem):
    s, t, f = lax.axis_index("src"), lax.axis_index("tgt"), lax.axis_index("feat")
    x, zl = s // 2, s % 2
    y, c = f // 2, f % 2
    step = 1 - 2 * zl
    xf, xb, xo = (x + step + 4) % 4, (x - step + 4) % 4, (x + 2) % 4
    yf, yb, yo = (y + step + 4) % 4, (y - step + 4) % 4, (y + 2) % 4
    X_F, X_B = {"src": xf * 2 + zl}, {"src": xb * 2 + zl}
    Y_F, Y_B = {"feat": yf * 2 + c}, {"feat": yb * 2 + c}
    Z_P, C_P = {"src": x * 2 + 1 - zl}, {"feat": y * 2 + 1 - c}
    T_UP, T_DN = {"tgt": (t + 1) % 4}, {"tgt": (t + 3) % 4}

    oz = 1 - zl
    ys, xs = (y, yb, yf, yo), (x, xb, xf, xo)

    def rows(yy, cc, half=None):
        if half is None:
            return pl.ds(pl.multiple_of((2 * yy + cc) * 128, 128), 128)
        return pl.ds(pl.multiple_of((2 * yy + cc) * 128 + half * 64, 64), 64)

    def item(layer, xx, z, yy, half=None):
        return E.at[layer, rows(yy, c, half), pl.ds(pl.multiple_of((2 * xx + z) * 256, 256), 256)]

    def pair(layer, xx, yy, half=None):
        return E.at[layer, rows(yy, c, half), pl.ds(pl.multiple_of(xx * 512, 512), 512)]

    def line(layer, yy, cc):
        return E.at[layer, rows(yy, cc), :]

    sent = []

    def copy(name, src, dst, dev):
        i = IDS[name]
        return pltpu.make_async_remote_copy(
            src_ref=src, dst_ref=dst, send_sem=ssem.at[i], recv_sem=rsem.at[i],
            device_id=dev, device_id_type=MESH,
        )

    def send(name, src, dev, dst=None):
        d = copy(name, src, src if dst is None else dst, dev)
        d.start()
        sent.append(d)

    def got(name, ref):
        copy(name, ref, ref, C_P).wait_recv()

    own_cols = pl.ds(pl.multiple_of(s * 256, 256), 256)
    own = E.at[:, rows(y, c), own_cols]
    load_err = pltpu.make_async_copy(err, own, local.at[0])
    load_codes = pltpu.make_async_copy(codes.at[0], codes_v, local.at[1])
    load_dec = pltpu.make_async_copy(dec_hbm.at[0], dec, local.at[2])
    load_mask = pltpu.make_async_copy(mask.at[0], mask_v, local.at[3])
    load_err.start()
    load_codes.start()
    load_dec.start()
    load_mask.start()

    barrier = pltpu.get_barrier_semaphore()
    for dev in (X_F, X_B, Y_F, Y_B, Z_P, C_P, T_UP, T_DN):
        pl.semaphore_signal(barrier, inc=1, device_id=dev, device_id_type=MESH)
    pl.semaphore_wait(barrier, 8)
    load_err.wait()

    def first(layer, kind, where):
        ax, (fw, bw) = ("X", (X_F, X_B)) if layer == 0 else ("Y", (Y_F, Y_B))
        send(ax + "f" + kind, where, fw)
        send(ax + "b" + kind, where, bw)

    def second(layer, piece, where):
        ax, (fw, bw) = ("P", (Y_F, Y_B)) if layer == 0 else ("Q", (X_F, X_B))
        send(ax + "f" + piece, where, fw)
        send(ax + "b" + piece, where, bw)

    own0, own1 = item(0, x, zl, y), item(1, x, zl, y)
    send("Z0", own0, Z_P)
    send("Z1", own1, Z_P)
    first(0, "A", own0)
    first(1, "A", own1)
    second(1, "A", own1)
    second(0, "A", own0)

    load_codes.wait()
    for i in range(4):
        codes_t[i * 128 : (i + 1) * 128, :] = codes_v[:, i * 128 : (i + 1) * 128].T

    def first_relay(layer, kind):
        z = zl if kind == "A" else oz
        if layer == 0:
            got("Xf" + kind, item(0, xb, z, y))
            send("Xrf" + kind, item(0, xb, z, y, 0), X_F)
            got("Xb" + kind, item(0, xf, z, y))
            send("Xrb" + kind, item(0, xf, z, y, 1), X_B)
        else:
            got("Yf" + kind, item(1, x, z, yb))
            send("Yrf" + kind, item(1, x, z, yb, 0), Y_F)
            got("Yb" + kind, item(1, x, z, yf))
            send("Yrb" + kind, item(1, x, z, yf, 1), Y_B)

    def first_rest(layer):
        for kind, z in (("A", zl), ("Z", oz)):
            if layer == 0:
                got("Xrf" + kind, item(0, xo, z, y, 0))
                got("Xrb" + kind, item(0, xo, z, y, 1))
            else:
                got("Yrf" + kind, item(1, x, z, yo, 0))
                got("Yrb" + kind, item(1, x, z, yo, 1))

    def piece_at(layer, piece, near, half=None):
        if piece in "AZ":
            z = zl if piece == "A" else oz
            return item(0, x, z, near, half) if layer == 0 else item(1, near, z, y, half)
        i = int(piece)
        return pair(0, xs[i], near, half) if layer == 0 else pair(1, near, ys[i], half)

    def second_relay(layer, piece):
        ax, (fw, bw), (nb, nf) = ("P", (Y_F, Y_B), (yb, yf)) if layer == 0 else ("Q", (X_F, X_B), (xb, xf))
        got(ax + "f" + piece, piece_at(layer, piece, nb))
        send(ax + "rf" + piece, piece_at(layer, piece, nb, 0), fw)
        got(ax + "b" + piece, piece_at(layer, piece, nf))
        send(ax + "rb" + piece, piece_at(layer, piece, nf, 1), bw)

    def second_rest(layer, piece):
        ax, far = ("P", yo) if layer == 0 else ("Q", xo)
        got(ax + "rf" + piece, piece_at(layer, piece, far, 0))
        got(ax + "rb" + piece, piece_at(layer, piece, far, 1))

    got("Z0", item(0, x, oz, y))
    first(0, "Z", item(0, x, oz, y))
    second(0, "Z", item(0, x, oz, y))
    first_relay(0, "A")
    first_relay(1, "A")
    got("Z1", item(1, x, oz, y))
    first(1, "Z", item(1, x, oz, y))
    second(1, "Z", item(1, x, oz, y))
    second_relay(1, "A")
    first_relay(0, "Z")
    second(0, "1", pair(0, xb, y))
    second(0, "2", pair(0, xf, y))
    first_relay(1, "Z")
    second_relay(1, "Z")
    second(1, "1", pair(1, x, yb))
    second(1, "2", pair(1, x, yf))
    first_rest(0)
    second(0, "3", pair(0, xo, y))
    send("D00", line(0, y, c), C_P)
    first_rest(1)
    second_rest(1, "A")
    second_rest(1, "Z")
    send("D10", line(1, y, c), C_P)

    live0, live1 = 2 * t >= s, 2 * t + 1 >= s

    def code_part(layer, k):
        block = pl.ds(pl.multiple_of(ys[k] * 256, 256), 256)
        for n in range(2):
            cols = slice(n * 256, (n + 1) * 256)

            def product():
                return lax.dot_general(
                    E[layer, block, :], dec[layer, cols, :], (((1,), (1,)), ((), ())),
                    preferred_element_type=jnp.float32,
                )

            if layer == 0:

                @pl.when(live0)
                def _():
                    part[k, :, cols] = product()

                @pl.when(jnp.logical_not(live0))
                def _():
                    part[k, :, cols] = jnp.zeros((256, 256), jnp.float32)
            else:

                @pl.when(live1)
                def _():
                    part[k, :, cols] += product()

    lo, hi = slice(0, 128), slice(128, 256)

    def push(i, value, dev):
        most = jnp.max(jnp.abs(value), axis=0, keepdims=True)
        fits = most > 1e-33
        inverse = jnp.where(fits, 32767.0 / jnp.where(fits, most, 1.0), 0.0)
        qout[i] = jnp.round(value * inverse).astype(jnp.int32).astype(jnp.int16)
        sout[i] = most * (1.0 / 32767.0)
        copy("S%d" % i, sout.at[i], sin.at[i], dev).start()
        copy("R%d" % i, qout.at[i], qin.at[i], dev).start()

    def pull(i):
        got("S%d" % i, sin.at[i])
        got("R%d" % i, qin.at[i])
        return qin[i].astype(jnp.int32).astype(jnp.float32) * sin[i]

    def reduce_start(k):
        d = (t - ys[k] + 4) % 4

        @pl.when(d == 2)
        def _():
            push(0, part[k, lo], T_DN)
            push(1, part[k, hi], T_UP)

        @pl.when(d == 1)
        def _():
            push(2, part[k, hi], T_DN)

        @pl.when(d == 3)
        def _():
            push(4, part[k, lo], T_UP)

    def reduce_next(k):
        d = (t - ys[k] + 4) % 4

        @pl.when(d == 1)
        def _():
            push(3, part[k, lo] + pull(0), T_DN)

        @pl.when(d == 3)
        def _():
            push(5, part[k, hi] + pull(1), T_UP)

    load_dec.wait()
    got("D00", line(0, y, 1 - c))
    code_part(0, 0)
    second_relay(0, "A")
    second_relay(0, "Z")
    second_relay(1, "1")
    got("D10", line(1, y, 1 - c))
    code_part(1, 0)
    reduce_start(0)
    second_relay(1, "2")
    second(1, "3", pair(1, x, yo))
    second_relay(0, "1")
    second_relay(0, "2")
    second_rest(1, "1")
    send("D11", line(1, yb, c), C_P)
    second_relay(0, "3")
    send("D01", line(0, yb, c), C_P)
    send("D02", line(0, yf, c), C_P)
    second_rest(1, "2")
    send("D12", line(1, yf, c), C_P)
    got("D01", line(0, yb, 1 - c))
    code_part(0, 1)
    second_relay(1, "3")
    got("D11", line(1, yb, 1 - c))
    code_part(1, 1)
    reduce_start(1)
    for piece in "AZ123":
        second_rest(0, piece)
    send("D03", line(0, yo, c), C_P)
    got("D02", line(0, yf, 1 - c))
    code_part(0, 2)
    second_rest(1, "3")
    send("D13", line(1, yo, c), C_P)
    got("D12", line(1, yf, 1 - c))
    code_part(1, 2)
    reduce_start(2)
    reduce_next(0)
    got("D03", line(0, yo, 1 - c))
    code_part(0, 3)
    got("D13", line(1, yo, 1 - c))
    code_part(1, 3)
    reduce_start(3)
    reduce_next(1)

    def tile_grads(layer, live):
        @pl.when(live)
        def _():
            def one(i, carry):
                cols = pl.ds(pl.multiple_of(i * 256, 256), 256)
                dw[0, layer, :, cols] = jnp.dot(
                    codes_t[...], E[layer, :, cols], preferred_element_type=jnp.float32
                ).astype(jnp.bfloat16)
                return carry

            lax.fori_loop(0, 8, one, 0)

        @pl.when(jnp.logical_not(live))
        def _():
            dw[0, layer] = jnp.zeros((512, 2048), jnp.bfloat16)

    tile_grads(0, live0)
    reduce_next(2)
    tile_grads(1, live1)
    reduce_next(3)

    load_mask.wait()
    for k in range(4):

        @pl.when(ys[k] == t)
        def _():
            low = part[k, lo] + pull(4) + pull(3)
            high = part[k, hi] + pull(2) + pull(5)
            cg[0, lo] = (low * mask_v[lo].astype(jnp.float32)).astype(jnp.bfloat16)
            cg[0, hi] = (high * mask_v[hi].astype(jnp.float32)).astype(jnp.bfloat16)

    for d in sent:
        d.wait_send()
    for i in range(6):
        copy("S%d" % i, sout.at[i], sin.at[i], C_P).wait_send()
        copy("R%d" % i, qout.at[i], qin.at[i], C_P).wait_send()


def body(errors, saved_codes, active_mask, decoder):
    n = len(NAMES)
    return pl.pallas_call(
        kernel,
        out_shape=(
            jax.ShapeDtypeStruct((1, 256, 512), jnp.bfloat16),
            jax.ShapeDtypeStruct((1, 2, 512, 2048), jnp.bfloat16),
        ),
        in_specs=[pl.BlockSpec(memory_space=pltpu.HBM)] * 4,
        out_specs=(pl.BlockSpec(memory_space=pltpu.VMEM),) * 2,
        scratch_shapes=[
            pltpu.VMEM((2, 1024, 2048), jnp.bfloat16),
            pltpu.VMEM((1024, 512), jnp.bfloat16),
            pltpu.VMEM((512, 1024), jnp.bfloat16),
            pltpu.VMEM((2, 512, 2048), jnp.bfloat16),
            pltpu.VMEM((256, 512), jnp.int32),
            pltpu.VMEM((4, 256, 512), jnp.float32),
            pltpu.VMEM((6, 128, 512), jnp.int16),
            pltpu.VMEM((6, 1, 512), jnp.float32),
            pltpu.VMEM((6, 128, 512), jnp.int16),
            pltpu.VMEM((6, 1, 512), jnp.float32),
            pltpu.SemaphoreType.DMA((4,)),
            pltpu.SemaphoreType.DMA((n,)),
            pltpu.SemaphoreType.DMA((n,)),
        ],
        compiler_params=pltpu.CompilerParams(
            collective_id=0, has_side_effects=True, vmem_limit_bytes=48 * 1024 * 1024
        ),
    )(*(pltpu.with_memory_space_constraint(a, pltpu.HBM) for a in (errors, saved_codes, active_mask, decoder)))


def solution(mesh):
    in_specs = (
        P("tgt", "feat", "src"),
        P("src", None, "feat"),
        P("src", "tgt", "feat"),
        P("src", "tgt", "feat", None),
    )
    out_specs = (P("src", "tgt", "feat"), P("src", "tgt", "feat", None))
    return jax.shard_map(body, mesh=mesh, in_specs=in_specs, out_specs=out_specs, check_vma=False)
```

```python
import jax
import jax.numpy as jnp
from jax import lax
from jax.experimental import pallas as pl
from jax.experimental.pallas import tpu as pltpu
from jax.sharding import PartitionSpec as P

MESH = pl.DeviceIdType.MESH

NAMES = (
    ["Z0", "Z1"]
    + [a + b for a in "XY" for b in ("fA", "bA", "rfA", "rbA", "Vf", "Vb", "Vo")]
    + [a + b + i for a in "PQ" for b in ("f", "b", "rf", "rb") for i in "AZ123"]
    + ["D" + str(layer) + str(k) for layer in range(2) for k in range(3)]
    + ["D" + str(layer) + "3" + str(i) for layer in range(2) for i in range(4)]
    + [a + str(i) for a in "RS" for i in range(12)]
)
IDS = {name: i for i, name in enumerate(NAMES)}


def kernel(err, codes, mask, dec_hbm, cg, dw, E, codes_v, codes_t, dec, mask_v, part, qout, sout, qin, sin, local, ssem, rsem):
    s, t, f = lax.axis_index("src"), lax.axis_index("tgt"), lax.axis_index("feat")
    x, zl = s // 2, s % 2
    y, c = f // 2, f % 2
    step = 1 - 2 * zl
    xf, xb, xo = (x + step + 4) % 4, (x - step + 4) % 4, (x + 2) % 4
    yf, yb, yo = (y + step + 4) % 4, (y - step + 4) % 4, (y + 2) % 4
    X_F, X_B = {"src": xf * 2 + zl}, {"src": xb * 2 + zl}
    Y_F, Y_B = {"feat": yf * 2 + c}, {"feat": yb * 2 + c}
    Z_P, C_P = {"src": x * 2 + 1 - zl}, {"feat": y * 2 + 1 - c}
    T_UP, T_DN = {"tgt": (t + 1) % 4}, {"tgt": (t + 3) % 4}

    oz = 1 - zl
    ys, xs = (y, yb, yf, yo), (x, xb, xf, xo)

    def rows(yy, cc, half=None):
        if half is None:
            return pl.ds(pl.multiple_of((2 * yy + cc) * 128, 128), 128)
        return pl.ds(pl.multiple_of((2 * yy + cc) * 128 + half * 64, 64), 64)

    def item(layer, xx, z, yy, half=None):
        return E.at[layer, rows(yy, c, half), pl.ds(pl.multiple_of((2 * xx + z) * 256, 256), 256)]

    def pair(layer, xx, yy, half=None):
        return E.at[layer, rows(yy, c, half), pl.ds(pl.multiple_of(xx * 512, 512), 512)]

    def line(layer, yy, cc):
        return E.at[layer, rows(yy, cc), :]

    sent = []

    def copy(name, src, dst, dev):
        i = IDS[name]
        return pltpu.make_async_remote_copy(
            src_ref=src, dst_ref=dst, send_sem=ssem.at[i], recv_sem=rsem.at[i],
            device_id=dev, device_id_type=MESH,
        )

    def send(name, src, dev, dst=None):
        d = copy(name, src, src if dst is None else dst, dev)
        d.start()
        sent.append(d)

    def got(name, ref):
        copy(name, ref, ref, C_P).wait_recv()

    own_cols = pl.ds(pl.multiple_of(s * 256, 256), 256)
    own = E.at[:, rows(y, c), own_cols]
    load_err = pltpu.make_async_copy(err, own, local.at[0])
    load_codes = pltpu.make_async_copy(codes.at[0], codes_v, local.at[1])
    load_dec = pltpu.make_async_copy(dec_hbm.at[0], dec, local.at[2])
    load_mask = pltpu.make_async_copy(mask.at[0], mask_v, local.at[3])
    load_err.start()
    load_codes.start()
    load_dec.start()
    load_mask.start()

    barrier = pltpu.get_barrier_semaphore()
    for dev in (X_F, X_B, Y_F, Y_B, Z_P, C_P, T_UP, T_DN):
        pl.semaphore_signal(barrier, inc=1, device_id=dev, device_id_type=MESH)
    pl.semaphore_wait(barrier, 8)
    load_err.wait()

    def first(layer, kind, where):
        ax, (fw, bw) = ("X", (X_F, X_B)) if layer == 0 else ("Y", (Y_F, Y_B))
        send(ax + "f" + kind, where, fw)
        send(ax + "b" + kind, where, bw)

    def second(layer, piece, where):
        ax, (fw, bw) = ("P", (Y_F, Y_B)) if layer == 0 else ("Q", (X_F, X_B))
        send(ax + "f" + piece, where, fw)
        send(ax + "b" + piece, where, bw)

    own0, own1 = item(0, x, zl, y), item(1, x, zl, y)
    send("Z0", own0, Z_P)
    send("Z1", own1, Z_P)
    first(0, "A", own0)
    first(1, "A", own1)
    second(1, "A", own1)
    second(0, "A", own0)

    load_codes.wait()
    for i in range(4):
        codes_t[i * 128 : (i + 1) * 128, :] = codes_v[:, i * 128 : (i + 1) * 128].T

    def first_relay(layer, way):
        if layer == 0:
            near, dev, half = (xb, X_F, 0) if way == "f" else (xf, X_B, 1)
            got("X" + way + "A", item(0, near, zl, y))
            send("Xr" + way + "A", item(0, near, zl, y, half), dev)
        else:
            near, dev, half = (yb, Y_F, 0) if way == "f" else (yf, Y_B, 1)
            got("Y" + way + "A", item(1, x, zl, near))
            send("Yr" + way + "A", item(1, x, zl, near, half), dev)

    def first_rest(layer):
        if layer == 0:
            got("XrfA", item(0, xo, zl, y, 0))
            got("XrbA", item(0, xo, zl, y, 1))
        else:
            got("YrfA", item(1, x, zl, yo, 0))
            got("YrbA", item(1, x, zl, yo, 1))

    def across(layer, way):
        if layer == 0:
            send("XV" + way, item(0, {"f": xb, "b": xf, "o": xo}[way], zl, y), Z_P)
        else:
            send("YV" + way, item(1, x, zl, {"f": yb, "b": yf, "o": yo}[way]), Z_P)

    def crossed(layer, way):
        if layer == 0:
            got("XV" + way, item(0, {"f": xf, "b": xb, "o": xo}[way], oz, y))
        else:
            got("YV" + way, item(1, x, oz, {"f": yf, "b": yb, "o": yo}[way]))

    def piece_at(layer, piece, near, half=None):
        if piece in "AZ":
            z = zl if piece == "A" else oz
            return item(0, x, z, near, half) if layer == 0 else item(1, near, z, y, half)
        i = int(piece)
        return pair(0, xs[i], near, half) if layer == 0 else pair(1, near, ys[i], half)

    def second_relay(layer, piece):
        ax, (fw, bw), (nb, nf) = ("P", (Y_F, Y_B), (yb, yf)) if layer == 0 else ("Q", (X_F, X_B), (xb, xf))
        got(ax + "f" + piece, piece_at(layer, piece, nb))
        send(ax + "rf" + piece, piece_at(layer, piece, nb, 0), fw)
        got(ax + "b" + piece, piece_at(layer, piece, nf))
        send(ax + "rb" + piece, piece_at(layer, piece, nf, 1), bw)

    def second_rest(layer, piece):
        ax, far = ("P", yo) if layer == 0 else ("Q", xo)
        got(ax + "rf" + piece, piece_at(layer, piece, far, 0))
        got(ax + "rb" + piece, piece_at(layer, piece, far, 1))

    got("Z0", item(0, x, oz, y))
    second(0, "Z", item(0, x, oz, y))
    first_relay(0, "f")
    across(0, "f")
    first_relay(0, "b")
    across(0, "b")
    first_relay(1, "f")
    across(1, "f")
    first_relay(1, "b")
    got("Z1", item(1, x, oz, y))
    second(1, "Z", item(1, x, oz, y))
    second_relay(1, "A")
    crossed(0, "f")
    second(0, "2", pair(0, xf, y))
    first_rest(0)
    across(0, "o")
    across(1, "b")
    second_relay(1, "Z")
    crossed(0, "b")
    second(0, "1", pair(0, xb, y))
    first_rest(1)
    across(1, "o")
    crossed(1, "f")
    second(1, "2", pair(1, x, yf))
    crossed(0, "o")
    second(0, "3", pair(0, xo, y))
    send("D00", line(0, y, c), C_P)
    crossed(1, "b")
    second(1, "1", pair(1, x, yb))
    second_rest(1, "A")
    second_rest(1, "Z")
    send("D10", line(1, y, c), C_P)
    crossed(1, "o")

    live0, live1 = 2 * t >= s, 2 * t + 1 >= s

    def code_part(layer, k):
        block = pl.ds(pl.multiple_of(ys[k] * 256, 256), 256)
        for n in range(2):
            cols = slice(n * 256, (n + 1) * 256)

            def product():
                return lax.dot_general(
                    E[layer, block, :], dec[layer, cols, :], (((1,), (1,)), ((), ())),
                    preferred_element_type=jnp.float32,
                )

            if layer == 0:

                @pl.when(live0)
                def _():
                    part[k, :, cols] = product()

                @pl.when(jnp.logical_not(live0))
                def _():
                    part[k, :, cols] = jnp.zeros((256, 256), jnp.float32)
            else:

                @pl.when(live1)
                def _():
                    part[k, :, cols] += product()

    def push(i, value, dev):
        most = jnp.max(jnp.abs(value), axis=0, keepdims=True)
        fits = most > 1e-33
        inverse = jnp.where(fits, 32767.0 / jnp.where(fits, most, 1.0), 0.0)
        qout[i] = jnp.round(value * inverse).astype(jnp.int32).astype(jnp.int16)
        sout[i] = most * (1.0 / 32767.0)
        copy("S%d" % i, sout.at[i], sin.at[i], dev).start()
        copy("R%d" % i, qout.at[i], qin.at[i], dev).start()

    def pull(i):
        got("S%d" % i, sin.at[i])
        got("R%d" % i, qin.at[i])
        return qin[i].astype(jnp.int32).astype(jnp.float32) * sin[i]

    los = (slice(0, 64), slice(64, 128))
    his = (slice(128, 192), slice(192, 256))

    def reduce_start(k):
        d = (t - ys[k] + 4) % 4

        @pl.when(d == 2)
        def _():
            for h in range(2):
                push(0 + h, part[k, los[h]], T_DN)
                push(2 + h, part[k, his[h]], T_UP)

        @pl.when(d == 1)
        def _():
            for h in range(2):
                push(4 + h, part[k, his[h]], T_DN)

        @pl.when(d == 3)
        def _():
            for h in range(2):
                push(8 + h, part[k, los[h]], T_UP)

    def reduce_next(k, halves=(0, 1)):
        d = (t - ys[k] + 4) % 4

        @pl.when(d == 1)
        def _():
            for h in halves:
                push(6 + h, part[k, los[h]] + pull(0 + h), T_DN)

        @pl.when(d == 3)
        def _():
            for h in halves:
                push(10 + h, part[k, his[h]] + pull(2 + h), T_UP)

    load_dec.wait()
    got("D00", line(0, y, 1 - c))
    code_part(0, 0)
    second_relay(0, "A")
    second_relay(0, "Z")
    second_relay(1, "2")
    got("D10", line(1, y, 1 - c))
    code_part(1, 0)
    reduce_start(0)
    second_relay(1, "1")
    second(1, "3", pair(1, x, yo))
    second_relay(0, "2")
    second_relay(0, "1")
    second_rest(1, "2")
    send("D12", line(1, yf, c), C_P)
    second_relay(0, "3")
    send("D02", line(0, yf, c), C_P)
    send("D01", line(0, yb, c), C_P)
    second_rest(1, "1")
    send("D11", line(1, yb, c), C_P)
    got("D02", line(0, yf, 1 - c))
    code_part(0, 2)
    second_relay(1, "3")
    got("D12", line(1, yf, 1 - c))
    code_part(1, 2)
    reduce_start(2)
    second_rest(0, "A")
    second_rest(0, "Z")
    send("D030", pair(0, x, yo), C_P)
    send("D130", pair(1, x, yo), C_P)
    send("D131", pair(1, xb, yo), C_P)
    send("D132", pair(1, xf, yo), C_P)
    got("D01", line(0, yb, 1 - c))
    code_part(0, 1)
    for i, piece in ((2, "2"), (1, "1"), (3, "3")):
        second_rest(0, piece)
        send("D03%d" % i, pair(0, xs[i], yo), C_P)
    second_rest(1, "3")
    send("D133", pair(1, xo, yo), C_P)
    got("D11", line(1, yb, 1 - c))
    code_part(1, 1)
    reduce_start(1)
    for i in (0, 2, 1, 3):
        got("D03%d" % i, E.at[0, rows(yo, 1 - c), pl.ds(pl.multiple_of(xs[i] * 512, 512), 512)])
    code_part(0, 3)
    for i in range(4):
        got("D13%d" % i, E.at[1, rows(yo, 1 - c), pl.ds(pl.multiple_of(xs[i] * 512, 512), 512)])
    code_part(1, 3)
    reduce_start(3)
    reduce_next(0)
    reduce_next(2)

    def tile_grads(layer, live, start, stop):
        @pl.when(live)
        def _():
            def one(i, carry):
                cols = pl.ds(pl.multiple_of(i * 256, 256), 256)
                dw[0, layer, :, cols] = jnp.dot(
                    codes_t[...], E[layer, :, cols], preferred_element_type=jnp.float32
                ).astype(jnp.bfloat16)
                return carry

            lax.fori_loop(start, stop, one, 0)

        @pl.when(jnp.logical_not(live))
        def _():
            dw[0, layer, :, start * 256 : stop * 256] = jnp.zeros((512, (stop - start) * 256), jnp.bfloat16)

    tile_grads(0, live0, 0, 4)
    reduce_next(1)
    tile_grads(0, live0, 4, 8)
    tile_grads(1, live1, 0, 3)
    reduce_next(3, (0,))
    reduce_next(3, (1,))
    tile_grads(1, live1, 3, 8)

    load_mask.wait()
    for k in range(4):

        @pl.when(ys[k] == t)
        def _():
            for h in range(2):
                low = part[k, los[h]] + pull(8 + h) + pull(6 + h)
                high = part[k, his[h]] + pull(4 + h) + pull(10 + h)
                cg[0, los[h]] = (low * mask_v[los[h]].astype(jnp.float32)).astype(jnp.bfloat16)
                cg[0, his[h]] = (high * mask_v[his[h]].astype(jnp.float32)).astype(jnp.bfloat16)

    for d in sent:
        d.wait_send()
    for i in range(12):
        copy("S%d" % i, sout.at[i], sin.at[i], C_P).wait_send()
        copy("R%d" % i, qout.at[i], qin.at[i], C_P).wait_send()


def body(errors, saved_codes, active_mask, decoder):
    n = len(NAMES)
    return pl.pallas_call(
        kernel,
        out_shape=(
            jax.ShapeDtypeStruct((1, 256, 512), jnp.bfloat16),
            jax.ShapeDtypeStruct((1, 2, 512, 2048), jnp.bfloat16),
        ),
        in_specs=[pl.BlockSpec(memory_space=pltpu.HBM)] * 4,
        out_specs=(pl.BlockSpec(memory_space=pltpu.VMEM),) * 2,
        scratch_shapes=[
            pltpu.VMEM((2, 1024, 2048), jnp.bfloat16),
            pltpu.VMEM((1024, 512), jnp.bfloat16),
            pltpu.VMEM((512, 1024), jnp.bfloat16),
            pltpu.VMEM((2, 512, 2048), jnp.bfloat16),
            pltpu.VMEM((256, 512), jnp.int32),
            pltpu.VMEM((4, 256, 512), jnp.float32),
            pltpu.VMEM((12, 64, 512), jnp.int16),
            pltpu.VMEM((12, 1, 512), jnp.float32),
            pltpu.VMEM((12, 64, 512), jnp.int16),
            pltpu.VMEM((12, 1, 512), jnp.float32),
            pltpu.SemaphoreType.DMA((4,)),
            pltpu.SemaphoreType.DMA((n,)),
            pltpu.SemaphoreType.DMA((n,)),
        ],
        compiler_params=pltpu.CompilerParams(
            collective_id=0, has_side_effects=True, vmem_limit_bytes=48 * 1024 * 1024
        ),
    )(*(pltpu.with_memory_space_constraint(a, pltpu.HBM) for a in (errors, saved_codes, active_mask, decoder)))


def solution(mesh):
    in_specs = (
        P("tgt", "feat", "src"),
        P("src", None, "feat"),
        P("src", "tgt", "feat"),
        P("src", "tgt", "feat", None),
    )
    out_specs = (P("src", "tgt", "feat"), P("src", "tgt", "feat", None))
    return jax.shard_map(body, mesh=mesh, in_specs=in_specs, out_specs=out_specs, check_vma=False)
```

```python
import jax
import jax.numpy as jnp
from jax import lax
from jax.experimental import pallas as pl
from jax.experimental.pallas import tpu as pltpu
from jax.sharding import PartitionSpec as P

MESH = pl.DeviceIdType.MESH

NAMES = (
    ["Z0", "Z1"]
    + [a + b for a in "XY" for b in ("fA", "bA", "rfA", "rbA", "Vf", "Vb", "Vo")]
    + [a + b + i for a in "PQ" for b in ("f", "b", "rf", "rb") for i in "AZ123"]
    + ["D00", "D10", "D11", "D12"]
    + [a + str(i) for a in ("D01", "D02", "D03", "D13") for i in range(4)]
    + [a + str(i) for a in "RS" for i in range(12)]
)
IDS = {name: i for i, name in enumerate(NAMES)}


def kernel(err, codes, mask, dec_hbm, cg, dw, E, codes_v, codes_t, dec, mask_v, part, qout, sout, qin, sin, local, ssem, rsem):
    s, t, f = lax.axis_index("src"), lax.axis_index("tgt"), lax.axis_index("feat")
    x, zl = s // 2, s % 2
    y, c = f // 2, f % 2
    step = 1 - 2 * zl
    xf, xb, xo = (x + step + 4) % 4, (x - step + 4) % 4, (x + 2) % 4
    yf, yb, yo = (y + step + 4) % 4, (y - step + 4) % 4, (y + 2) % 4
    X_F, X_B = {"src": xf * 2 + zl}, {"src": xb * 2 + zl}
    Y_F, Y_B = {"feat": yf * 2 + c}, {"feat": yb * 2 + c}
    Z_P, C_P = {"src": x * 2 + 1 - zl}, {"feat": y * 2 + 1 - c}
    T_UP, T_DN = {"tgt": (t + 1) % 4}, {"tgt": (t + 3) % 4}

    oz = 1 - zl
    ys, xs = (y, yb, yf, yo), (x, xb, xf, xo)

    def rows(yy, cc, half=None):
        if half is None:
            return pl.ds(pl.multiple_of((2 * yy + cc) * 128, 128), 128)
        return pl.ds(pl.multiple_of((2 * yy + cc) * 128 + half * 64, 64), 64)

    def item(layer, xx, z, yy, half=None):
        return E.at[layer, rows(yy, c, half), pl.ds(pl.multiple_of((2 * xx + z) * 256, 256), 256)]

    def pair(layer, xx, yy, half=None):
        return E.at[layer, rows(yy, c, half), pl.ds(pl.multiple_of(xx * 512, 512), 512)]

    def line(layer, yy, cc):
        return E.at[layer, rows(yy, cc), :]

    sent = []

    def copy(name, src, dst, dev):
        i = IDS[name]
        return pltpu.make_async_remote_copy(
            src_ref=src, dst_ref=dst, send_sem=ssem.at[i], recv_sem=rsem.at[i],
            device_id=dev, device_id_type=MESH,
        )

    def send(name, src, dev, dst=None):
        d = copy(name, src, src if dst is None else dst, dev)
        d.start()
        sent.append(d)

    def got(name, ref):
        copy(name, ref, ref, C_P).wait_recv()

    own_cols = pl.ds(pl.multiple_of(s * 256, 256), 256)
    own = E.at[:, rows(y, c), own_cols]
    load_err = pltpu.make_async_copy(err, own, local.at[0])
    load_codes = pltpu.make_async_copy(codes.at[0], codes_v, local.at[1])
    load_dec = pltpu.make_async_copy(dec_hbm.at[0], dec, local.at[2])
    load_mask = pltpu.make_async_copy(mask.at[0], mask_v, local.at[3])
    load_err.start()
    load_codes.start()
    load_dec.start()
    load_mask.start()

    barrier = pltpu.get_barrier_semaphore()
    for dev in (X_F, X_B, Y_F, Y_B, Z_P, C_P, T_UP, T_DN):
        pl.semaphore_signal(barrier, inc=1, device_id=dev, device_id_type=MESH)
    pl.semaphore_wait(barrier, 8)
    load_err.wait()

    def first(layer, kind, where):
        ax, (fw, bw) = ("X", (X_F, X_B)) if layer == 0 else ("Y", (Y_F, Y_B))
        send(ax + "f" + kind, where, fw)
        send(ax + "b" + kind, where, bw)

    def second(layer, piece, where):
        ax, (fw, bw) = ("P", (Y_F, Y_B)) if layer == 0 else ("Q", (X_F, X_B))
        send(ax + "f" + piece, where, fw)
        send(ax + "b" + piece, where, bw)

    own0, own1 = item(0, x, zl, y), item(1, x, zl, y)
    send("Z0", own0, Z_P)
    send("Z1", own1, Z_P)
    first(0, "A", own0)
    first(1, "A", own1)
    second(1, "A", own1)
    second(0, "A", own0)

    load_codes.wait()
    for i in range(4):
        codes_t[i * 128 : (i + 1) * 128, :] = codes_v[:, i * 128 : (i + 1) * 128].T

    def first_relay(layer, way):
        if layer == 0:
            near, dev, half = (xb, X_F, 0) if way == "f" else (xf, X_B, 1)
            got("X" + way + "A", item(0, near, zl, y))
            send("Xr" + way + "A", item(0, near, zl, y, half), dev)
        else:
            near, dev, half = (yb, Y_F, 0) if way == "f" else (yf, Y_B, 1)
            got("Y" + way + "A", item(1, x, zl, near))
            send("Yr" + way + "A", item(1, x, zl, near, half), dev)

    def first_rest(layer):
        if layer == 0:
            got("XrfA", item(0, xo, zl, y, 0))
            got("XrbA", item(0, xo, zl, y, 1))
        else:
            got("YrfA", item(1, x, zl, yo, 0))
            got("YrbA", item(1, x, zl, yo, 1))

    def across(layer, way):
        if layer == 0:
            send("XV" + way, item(0, {"f": xb, "b": xf, "o": xo}[way], zl, y), Z_P)
        else:
            send("YV" + way, item(1, x, zl, {"f": yb, "b": yf, "o": yo}[way]), Z_P)

    def crossed(layer, way):
        if layer == 0:
            got("XV" + way, item(0, {"f": xf, "b": xb, "o": xo}[way], oz, y))
        else:
            got("YV" + way, item(1, x, oz, {"f": yf, "b": yb, "o": yo}[way]))

    def piece_at(layer, piece, near, half=None):
        if piece in "AZ":
            z = zl if piece == "A" else oz
            return item(0, x, z, near, half) if layer == 0 else item(1, near, z, y, half)
        i = int(piece)
        return pair(0, xs[i], near, half) if layer == 0 else pair(1, near, ys[i], half)

    def second_relay(layer, piece):
        ax, (fw, bw), (nb, nf) = ("P", (Y_F, Y_B), (yb, yf)) if layer == 0 else ("Q", (X_F, X_B), (xb, xf))
        got(ax + "f" + piece, piece_at(layer, piece, nb))
        send(ax + "rf" + piece, piece_at(layer, piece, nb, 0), fw)
        got(ax + "b" + piece, piece_at(layer, piece, nf))
        send(ax + "rb" + piece, piece_at(layer, piece, nf, 1), bw)

    def second_rest(layer, piece):
        ax, far = ("P", yo) if layer == 0 else ("Q", xo)
        got(ax + "rf" + piece, piece_at(layer, piece, far, 0))
        got(ax + "rb" + piece, piece_at(layer, piece, far, 1))

    got("Z0", item(0, x, oz, y))
    second(0, "Z", item(0, x, oz, y))
    first_relay(0, "f")
    across(0, "f")
    first_relay(0, "b")
    across(0, "b")
    first_relay(1, "f")
    across(1, "f")
    first_relay(1, "b")
    got("Z1", item(1, x, oz, y))
    second(1, "Z", item(1, x, oz, y))
    second_relay(1, "A")
    crossed(0, "f")
    second(0, "2", pair(0, xf, y))
    first_rest(0)
    across(0, "o")
    across(1, "b")
    second_relay(1, "Z")
    crossed(0, "b")
    second(0, "1", pair(0, xb, y))
    first_rest(1)
    across(1, "o")
    crossed(1, "f")
    second(1, "2", pair(1, x, yf))
    crossed(0, "o")
    second(0, "3", pair(0, xo, y))
    send("D00", line(0, y, c), C_P)
    crossed(1, "b")
    second(1, "1", pair(1, x, yb))
    second_rest(1, "A")
    second_rest(1, "Z")
    send("D10", line(1, y, c), C_P)
    crossed(1, "o")

    live0, live1 = 2 * t >= s, 2 * t + 1 >= s

    def code_part(layer, k, opening):
        block = pl.ds(pl.multiple_of(ys[k] * 256, 256), 256)
        for n in range(2):
            cols = slice(n * 256, (n + 1) * 256)

            def product():
                return lax.dot_general(
                    E[layer, block, :], dec[layer, cols, :], (((1,), (1,)), ((), ())),
                    preferred_element_type=jnp.float32,
                )

            live = (live0, live1)[layer]

            if opening:

                @pl.when(live)
                def _():
                    part[k, :, cols] = product()

                @pl.when(jnp.logical_not(live))
                def _():
                    part[k, :, cols] = jnp.zeros((256, 256), jnp.float32)
            else:

                @pl.when(live)
                def _():
                    part[k, :, cols] += product()

    def push(i, value, dev):
        most = jnp.max(jnp.abs(value), axis=0, keepdims=True)
        fits = most > 1e-33
        inverse = jnp.where(fits, 32767.0 / jnp.where(fits, most, 1.0), 0.0)
        qout[i] = jnp.round(value * inverse).astype(jnp.int32).astype(jnp.int16)
        sout[i] = most * (1.0 / 32767.0)
        copy("S%d" % i, sout.at[i], sin.at[i], dev).start()
        copy("R%d" % i, qout.at[i], qin.at[i], dev).start()

    def pull(i):
        got("S%d" % i, sin.at[i])
        got("R%d" % i, qin.at[i])
        return qin[i].astype(jnp.int32).astype(jnp.float32) * sin[i]

    los = (slice(0, 64), slice(64, 128))
    his = (slice(128, 192), slice(192, 256))

    def reduce_start(k):
        d = (t - ys[k] + 4) % 4

        @pl.when(d == 2)
        def _():
            for h in range(2):
                push(0 + h, part[k, los[h]], T_DN)
                push(2 + h, part[k, his[h]], T_UP)

        @pl.when(d == 1)
        def _():
            for h in range(2):
                push(4 + h, part[k, his[h]], T_DN)

        @pl.when(d == 3)
        def _():
            for h in range(2):
                push(8 + h, part[k, los[h]], T_UP)

    def reduce_next(k, halves=(0, 1)):
        d = (t - ys[k] + 4) % 4

        @pl.when(d == 1)
        def _():
            for h in halves:
                push(6 + h, part[k, los[h]] + pull(0 + h), T_DN)

        @pl.when(d == 3)
        def _():
            for h in halves:
                push(10 + h, part[k, his[h]] + pull(2 + h), T_UP)

    def chip_rows(i):
        send("D02%d" % i, pair(0, xs[i], yf), C_P)
        send("D01%d" % i, pair(0, xs[i], yb), C_P)

    def partner_pairs(layer, k, order):
        for i in order:
            got("D%d%d%d" % (layer, k, i), E.at[layer, rows(ys[k], 1 - c), pl.ds(pl.multiple_of(xs[i] * 512, 512), 512)])

    load_dec.wait()
    got("D00", line(0, y, 1 - c))
    code_part(0, 0, True)
    second_relay(0, "A")
    second_relay(0, "Z")
    chip_rows(0)
    second_relay(1, "2")
    got("D10", line(1, y, 1 - c))
    code_part(1, 0, False)
    reduce_start(0)
    second_relay(1, "1")
    second(1, "3", pair(1, x, yo))
    second_relay(0, "2")
    chip_rows(2)
    second_relay(0, "1")
    chip_rows(1)
    second_rest(1, "2")
    send("D12", line(1, yf, c), C_P)
    second_rest(1, "1")
    send("D11", line(1, yb, c), C_P)
    got("D12", line(1, yf, 1 - c))
    code_part(1, 2, True)
    second_relay(0, "3")
    chip_rows(3)
    got("D11", line(1, yb, 1 - c))
    code_part(1, 1, True)
    second_relay(1, "3")
    partner_pairs(0, 2, (0, 2, 1, 3))
    code_part(0, 2, False)
    reduce_start(2)
    partner_pairs(0, 1, (0, 2, 1, 3))
    code_part(0, 1, False)
    reduce_start(1)
    second_rest(0, "A")
    second_rest(0, "Z")
    send("D030", pair(0, x, yo), C_P)
    send("D130", pair(1, x, yo), C_P)
    send("D131", pair(1, xb, yo), C_P)
    send("D132", pair(1, xf, yo), C_P)
    for i, piece in ((2, "2"), (1, "1")):
        second_rest(0, piece)
        send("D03%d" % i, pair(0, xs[i], yo), C_P)
    second_rest(1, "3")
    send("D133", pair(1, xo, yo), C_P)
    second_rest(0, "3")
    send("D033", pair(0, xo, yo), C_P)
    partner_pairs(1, 3, range(4))
    code_part(1, 3, True)
    partner_pairs(0, 3, (0, 2, 1, 3))
    code_part(0, 3, False)
    reduce_start(3)
    reduce_next(0)
    reduce_next(2)

    def tile_grads(layer, live, start, stop):
        @pl.when(live)
        def _():
            def one(i, carry):
                cols = pl.ds(pl.multiple_of(i * 256, 256), 256)
                dw[0, layer, :, cols] = jnp.dot(
                    codes_t[...], E[layer, :, cols], preferred_element_type=jnp.float32
                ).astype(jnp.bfloat16)
                return carry

            lax.fori_loop(start, stop, one, 0)

        @pl.when(jnp.logical_not(live))
        def _():
            dw[0, layer, :, start * 256 : stop * 256] = jnp.zeros((512, (stop - start) * 256), jnp.bfloat16)

    tile_grads(0, live0, 0, 4)
    reduce_next(1)
    tile_grads(0, live0, 4, 8)
    tile_grads(1, live1, 0, 3)
    reduce_next(3, (0,))
    reduce_next(3, (1,))
    tile_grads(1, live1, 3, 8)

    load_mask.wait()
    for k in range(4):

        @pl.when(ys[k] == t)
        def _():
            for h in range(2):
                low = part[k, los[h]] + pull(8 + h) + pull(6 + h)
                high = part[k, his[h]] + pull(4 + h) + pull(10 + h)
                cg[0, los[h]] = (low * mask_v[los[h]].astype(jnp.float32)).astype(jnp.bfloat16)
                cg[0, his[h]] = (high * mask_v[his[h]].astype(jnp.float32)).astype(jnp.bfloat16)

    for d in sent:
        d.wait_send()
    for i in range(12):
        copy("S%d" % i, sout.at[i], sin.at[i], C_P).wait_send()
        copy("R%d" % i, qout.at[i], qin.at[i], C_P).wait_send()


def write_out(cg_v, dw_v, cg, dw, sems):
    copies = [pltpu.make_async_copy(cg_v, cg, sems.at[8])]
    for i in range(8):
        at = (0, i // 4, pl.ds(i % 4 * 128, 128))
        copies.append(pltpu.make_async_copy(dw_v.at[at], dw.at[at], sems.at[i]))
    for d in copies:
        d.start()
    for d in copies:
        d.wait()


def body(errors, saved_codes, active_mask, decoder):
    n = len(NAMES)
    results_shape = (
        jax.ShapeDtypeStruct((1, 256, 512), jnp.bfloat16),
        jax.ShapeDtypeStruct((1, 2, 512, 2048), jnp.bfloat16),
    )
    results = pl.pallas_call(
        kernel,
        out_shape=results_shape,
        in_specs=[pl.BlockSpec(memory_space=pltpu.HBM)] * 4,
        out_specs=(pl.BlockSpec(memory_space=pltpu.VMEM),) * 2,
        scratch_shapes=[
            pltpu.VMEM((2, 1024, 2048), jnp.bfloat16),
            pltpu.VMEM((1024, 512), jnp.bfloat16),
            pltpu.VMEM((512, 1024), jnp.bfloat16),
            pltpu.VMEM((2, 512, 2048), jnp.bfloat16),
            pltpu.VMEM((256, 512), jnp.int32),
            pltpu.VMEM((4, 256, 512), jnp.float32),
            pltpu.VMEM((12, 64, 512), jnp.int16),
            pltpu.VMEM((12, 1, 512), jnp.float32),
            pltpu.VMEM((12, 64, 512), jnp.int16),
            pltpu.VMEM((12, 1, 512), jnp.float32),
            pltpu.SemaphoreType.DMA((4,)),
            pltpu.SemaphoreType.DMA((n,)),
            pltpu.SemaphoreType.DMA((n,)),
        ],
        compiler_params=pltpu.CompilerParams(
            collective_id=0, has_side_effects=True, vmem_limit_bytes=48 * 1024 * 1024
        ),
    )(*(pltpu.with_memory_space_constraint(a, pltpu.HBM) for a in (errors, saved_codes, active_mask, decoder)))
    return pl.pallas_call(
        write_out,
        out_shape=results_shape,
        in_specs=[pl.BlockSpec(memory_space=pltpu.VMEM)] * 2,
        out_specs=(pl.BlockSpec(memory_space=pl.ANY),) * 2,
        scratch_shapes=[pltpu.SemaphoreType.DMA((9,))],
        compiler_params=pltpu.CompilerParams(vmem_limit_bytes=8 * 1024 * 1024),
    )(*results)


def solution(mesh):
    in_specs = (
        P("tgt", "feat", "src"),
        P("src", None, "feat"),
        P("src", "tgt", "feat"),
        P("src", "tgt", "feat", None),
    )
    out_specs = (P("src", "tgt", "feat"), P("src", "tgt", "feat", None))
    return jax.shard_map(body, mesh=mesh, in_specs=in_specs, out_specs=out_specs, check_vma=False)
```

```python
import jax
import jax.numpy as jnp
from jax import lax
from jax.experimental import pallas as pl
from jax.experimental.pallas import tpu as pltpu
from jax.sharding import PartitionSpec as P

MESH = pl.DeviceIdType.MESH

NAMES = (
    ["Z0", "Z1"]
    + [a + b for a in "XY" for b in ("fA", "bA", "rfA", "rbA", "Vf", "Vb", "Vo")]
    + [a + b + i for a in "PQ" for b in ("f", "b", "rf", "rb") for i in "AZ123"]
    + ["D00", "D10", "D11", "D12"]
    + [a + str(i) for a in ("D01", "D02", "D03", "D13") for i in range(4)]
    + [a + str(i) for a in "RS" for i in range(12)]
)
IDS = {name: i for i, name in enumerate(NAMES)}


def kernel(err, codes, mask, dec_hbm, cg, dw, E, codes_v, codes_t, dec, mask_v, part, qout, sout, qin, sin, local, ssem, rsem):
    s, t, f = lax.axis_index("src"), lax.axis_index("tgt"), lax.axis_index("feat")
    x, zl = s // 2, s % 2
    y, c = f // 2, f % 2
    step = 1 - 2 * zl
    xf, xb, xo = (x + step + 4) % 4, (x - step + 4) % 4, (x + 2) % 4
    yf, yb, yo = (y + step + 4) % 4, (y - step + 4) % 4, (y + 2) % 4
    X_F, X_B = {"src": xf * 2 + zl}, {"src": xb * 2 + zl}
    Y_F, Y_B = {"feat": yf * 2 + c}, {"feat": yb * 2 + c}
    Z_P, C_P = {"src": x * 2 + 1 - zl}, {"feat": y * 2 + 1 - c}
    T_UP, T_DN = {"tgt": (t + 1) % 4}, {"tgt": (t + 3) % 4}

    oz = 1 - zl
    ys, xs = (y, yb, yf, yo), (x, xb, xf, xo)

    def rows(yy, cc, half=None):
        if half is None:
            return pl.ds(pl.multiple_of((2 * yy + cc) * 128, 128), 128)
        return pl.ds(pl.multiple_of((2 * yy + cc) * 128 + half * 64, 64), 64)

    def item(layer, xx, z, yy, half=None):
        return E.at[layer, rows(yy, c, half), pl.ds(pl.multiple_of((2 * xx + z) * 256, 256), 256)]

    def pair(layer, xx, yy, half=None):
        return E.at[layer, rows(yy, c, half), pl.ds(pl.multiple_of(xx * 512, 512), 512)]

    def line(layer, yy, cc):
        return E.at[layer, rows(yy, cc), :]

    sent = []

    def copy(name, src, dst, dev):
        i = IDS[name]
        return pltpu.make_async_remote_copy(
            src_ref=src, dst_ref=dst, send_sem=ssem.at[i], recv_sem=rsem.at[i],
            device_id=dev, device_id_type=MESH,
        )

    def send(name, src, dev, dst=None):
        d = copy(name, src, src if dst is None else dst, dev)
        d.start()
        sent.append(d)

    def got(name, ref):
        copy(name, ref, ref, C_P).wait_recv()

    own_cols = pl.ds(pl.multiple_of(s * 256, 256), 256)
    own = E.at[:, rows(y, c), own_cols]
    load_err = pltpu.make_async_copy(err, own, local.at[0])
    load_codes = pltpu.make_async_copy(codes.at[0], codes_v, local.at[1])
    load_dec = pltpu.make_async_copy(dec_hbm.at[0], dec, local.at[2])
    load_mask = pltpu.make_async_copy(mask.at[0], mask_v, local.at[3])
    load_err.start()
    load_codes.start()
    load_dec.start()
    load_mask.start()

    barrier = pltpu.get_barrier_semaphore()
    for dev in (X_F, X_B, Y_F, Y_B, Z_P, C_P, T_UP, T_DN):
        pl.semaphore_signal(barrier, inc=1, device_id=dev, device_id_type=MESH)
    pl.semaphore_wait(barrier, 8)
    load_err.wait()

    def first(layer, kind, where):
        ax, (fw, bw) = ("X", (X_F, X_B)) if layer == 0 else ("Y", (Y_F, Y_B))
        send(ax + "f" + kind, where, fw)
        send(ax + "b" + kind, where, bw)

    def second(layer, piece, where):
        ax, (fw, bw) = ("P", (Y_F, Y_B)) if layer == 0 else ("Q", (X_F, X_B))
        send(ax + "f" + piece, where, fw)
        send(ax + "b" + piece, where, bw)

    own0, own1 = item(0, x, zl, y), item(1, x, zl, y)
    send("Z0", own0, Z_P)
    send("Z1", own1, Z_P)
    first(0, "A", own0)
    first(1, "A", own1)
    second(1, "A", own1)
    second(0, "A", own0)

    load_codes.wait()
    for i in range(4):
        codes_t[i * 128 : (i + 1) * 128, :] = codes_v[:, i * 128 : (i + 1) * 128].T

    def first_relay(layer, way):
        if layer == 0:
            near, dev, half = (xb, X_F, 0) if way == "f" else (xf, X_B, 1)
            got("X" + way + "A", item(0, near, zl, y))
            send("Xr" + way + "A", item(0, near, zl, y, half), dev)
        else:
            near, dev, half = (yb, Y_F, 0) if way == "f" else (yf, Y_B, 1)
            got("Y" + way + "A", item(1, x, zl, near))
            send("Yr" + way + "A", item(1, x, zl, near, half), dev)

    def first_rest(layer):
        if layer == 0:
            got("XrfA", item(0, xo, zl, y, 0))
            got("XrbA", item(0, xo, zl, y, 1))
        else:
            got("YrfA", item(1, x, zl, yo, 0))
            got("YrbA", item(1, x, zl, yo, 1))

    def across(layer, way):
        if layer == 0:
            send("XV" + way, item(0, {"f": xb, "b": xf, "o": xo}[way], zl, y), Z_P)
        else:
            send("YV" + way, item(1, x, zl, {"f": yb, "b": yf, "o": yo}[way]), Z_P)

    def crossed(layer, way):
        if layer == 0:
            got("XV" + way, item(0, {"f": xf, "b": xb, "o": xo}[way], oz, y))
        else:
            got("YV" + way, item(1, x, oz, {"f": yf, "b": yb, "o": yo}[way]))

    def piece_at(layer, piece, near, half=None):
        if piece in "AZ":
            z = zl if piece == "A" else oz
            return item(0, x, z, near, half) if layer == 0 else item(1, near, z, y, half)
        i = int(piece)
        return pair(0, xs[i], near, half) if layer == 0 else pair(1, near, ys[i], half)

    def second_relay(layer, piece):
        ax, (fw, bw), (nb, nf) = ("P", (Y_F, Y_B), (yb, yf)) if layer == 0 else ("Q", (X_F, X_B), (xb, xf))
        got(ax + "f" + piece, piece_at(layer, piece, nb))
        send(ax + "rf" + piece, piece_at(layer, piece, nb, 0), fw)
        got(ax + "b" + piece, piece_at(layer, piece, nf))
        send(ax + "rb" + piece, piece_at(layer, piece, nf, 1), bw)

    def second_rest(layer, piece):
        ax, far = ("P", yo) if layer == 0 else ("Q", xo)
        got(ax + "rf" + piece, piece_at(layer, piece, far, 0))
        got(ax + "rb" + piece, piece_at(layer, piece, far, 1))

    got("Z0", item(0, x, oz, y))
    second(0, "Z", item(0, x, oz, y))
    first_relay(0, "f")
    across(0, "f")
    first_relay(0, "b")
    across(0, "b")
    first_relay(1, "f")
    across(1, "f")
    first_relay(1, "b")
    got("Z1", item(1, x, oz, y))
    second(1, "Z", item(1, x, oz, y))
    second_relay(1, "A")
    crossed(0, "f")
    second(0, "2", pair(0, xf, y))
    first_rest(0)
    across(0, "o")
    across(1, "b")
    second_relay(1, "Z")
    crossed(0, "b")
    second(0, "1", pair(0, xb, y))
    first_rest(1)
    across(1, "o")
    crossed(1, "f")
    second(1, "2", pair(1, x, yf))
    crossed(0, "o")
    second(0, "3", pair(0, xo, y))
    send("D00", line(0, y, c), C_P)
    crossed(1, "b")
    second(1, "1", pair(1, x, yb))
    second_rest(1, "A")
    second_rest(1, "Z")
    send("D10", line(1, y, c), C_P)
    crossed(1, "o")

    live0, live1 = 2 * t >= s, 2 * t + 1 >= s

    def code_part(layer, k, opening):
        block = pl.ds(pl.multiple_of(ys[k] * 256, 256), 256)
        def product():
            return lax.dot_general(
                E[layer, block, :], dec[layer], (((1,), (1,)), ((), ())),
                preferred_element_type=jnp.float32,
            )

        live = (live0, live1)[layer]

        if opening:

            @pl.when(live)
            def _():
                part[k] = product()

            @pl.when(jnp.logical_not(live))
            def _():
                part[k] = jnp.zeros((256, 512), jnp.float32)
        else:

            @pl.when(live)
            def _():
                part[k] += product()

    def push(i, value, dev):
        most = jnp.max(jnp.abs(value), axis=0, keepdims=True)
        fits = most > 1e-33
        inverse = jnp.where(fits, 32767.0 / jnp.where(fits, most, 1.0), 0.0)
        qout[i] = jnp.round(value * inverse).astype(jnp.int32).astype(jnp.int16)
        sout[i] = most * (1.0 / 32767.0)
        copy("S%d" % i, sout.at[i], sin.at[i], dev).start()
        copy("R%d" % i, qout.at[i], qin.at[i], dev).start()

    def pull(i):
        got("S%d" % i, sin.at[i])
        got("R%d" % i, qin.at[i])
        return qin[i].astype(jnp.int32).astype(jnp.float32) * sin[i]

    los = (slice(0, 64), slice(64, 128))
    his = (slice(128, 192), slice(192, 256))

    def reduce_start(k):
        d = (t - ys[k] + 4) % 4

        @pl.when(d == 2)
        def _():
            for h in range(2):
                push(0 + h, part[k, los[h]], T_DN)
                push(2 + h, part[k, his[h]], T_UP)

        @pl.when(d == 1)
        def _():
            for h in range(2):
                push(4 + h, part[k, his[h]], T_DN)

        @pl.when(d == 3)
        def _():
            for h in range(2):
                push(8 + h, part[k, los[h]], T_UP)

    def reduce_next(k, halves=(0, 1)):
        d = (t - ys[k] + 4) % 4

        @pl.when(d == 1)
        def _():
            for h in halves:
                push(6 + h, part[k, los[h]] + pull(0 + h), T_DN)

        @pl.when(d == 3)
        def _():
            for h in halves:
                push(10 + h, part[k, his[h]] + pull(2 + h), T_UP)

    def chip_rows(i):
        send("D02%d" % i, pair(0, xs[i], yf), C_P)
        send("D01%d" % i, pair(0, xs[i], yb), C_P)

    def partner_pairs(layer, k, order):
        for i in order:
            got("D%d%d%d" % (layer, k, i), E.at[layer, rows(ys[k], 1 - c), pl.ds(pl.multiple_of(xs[i] * 512, 512), 512)])

    load_dec.wait()
    got("D00", line(0, y, 1 - c))
    code_part(0, 0, True)
    second_relay(0, "A")
    second_relay(0, "Z")
    chip_rows(0)
    second_relay(1, "2")
    got("D10", line(1, y, 1 - c))
    code_part(1, 0, False)
    reduce_start(0)
    second_relay(1, "1")
    second(1, "3", pair(1, x, yo))
    second_relay(0, "2")
    chip_rows(2)
    second_relay(0, "1")
    chip_rows(1)
    second_rest(1, "2")
    send("D12", line(1, yf, c), C_P)
    second_rest(1, "1")
    send("D11", line(1, yb, c), C_P)
    got("D12", line(1, yf, 1 - c))
    code_part(1, 2, True)
    second_relay(0, "3")
    chip_rows(3)
    got("D11", line(1, yb, 1 - c))
    code_part(1, 1, True)
    second_relay(1, "3")
    partner_pairs(0, 2, (0, 2, 1, 3))
    code_part(0, 2, False)
    reduce_start(2)
    partner_pairs(0, 1, (0, 2, 1, 3))
    code_part(0, 1, False)
    reduce_start(1)
    second_rest(0, "A")
    second_rest(0, "Z")
    send("D030", pair(0, x, yo), C_P)
    send("D130", pair(1, x, yo), C_P)
    send("D131", pair(1, xb, yo), C_P)
    send("D132", pair(1, xf, yo), C_P)
    for i, piece in ((2, "2"), (1, "1")):
        second_rest(0, piece)
        send("D03%d" % i, pair(0, xs[i], yo), C_P)
    second_rest(1, "3")
    send("D133", pair(1, xo, yo), C_P)
    second_rest(0, "3")
    send("D033", pair(0, xo, yo), C_P)
    partner_pairs(1, 3, range(4))
    code_part(1, 3, True)
    partner_pairs(0, 3, (0, 2, 1, 3))
    code_part(0, 3, False)
    reduce_start(3)
    reduce_next(2)
    reduce_next(1)
    reduce_next(0)

    def tile_grads(layer, live, start, stop):
        @pl.when(live)
        def _():
            def one(i, carry):
                cols = pl.ds(pl.multiple_of(i * 256, 256), 256)
                dw[0, layer, :, cols] = jnp.dot(
                    codes_t[...], E[layer, :, cols], preferred_element_type=jnp.float32
                ).astype(jnp.bfloat16)
                return carry

            lax.fori_loop(start, stop, one, 0)

        @pl.when(jnp.logical_not(live))
        def _():
            dw[0, layer, :, start * 256 : stop * 256] = jnp.zeros((512, (stop - start) * 256), jnp.bfloat16)

    tile_grads(0, live0, 0, 4)
    tile_grads(0, live0, 4, 8)
    tile_grads(1, live1, 0, 3)
    reduce_next(3, (0,))
    reduce_next(3, (1,))
    tile_grads(1, live1, 3, 8)

    load_mask.wait()
    for k in range(4):

        @pl.when(ys[k] == t)
        def _():
            for h in range(2):
                low = part[k, los[h]] + pull(8 + h) + pull(6 + h)
                high = part[k, his[h]] + pull(4 + h) + pull(10 + h)
                cg[0, los[h]] = (low * mask_v[los[h]].astype(jnp.float32)).astype(jnp.bfloat16)
                cg[0, his[h]] = (high * mask_v[his[h]].astype(jnp.float32)).astype(jnp.bfloat16)

    for d in sent:
        d.wait_send()
    for i in range(12):
        copy("S%d" % i, sout.at[i], sin.at[i], C_P).wait_send()
        copy("R%d" % i, qout.at[i], qin.at[i], C_P).wait_send()


def write_out(cg_v, dw_v, cg, dw, sems):
    copies = [pltpu.make_async_copy(cg_v, cg, sems.at[8])]
    for i in range(8):
        at = (0, i // 4, pl.ds(i % 4 * 128, 128))
        copies.append(pltpu.make_async_copy(dw_v.at[at], dw.at[at], sems.at[i]))
    for d in copies:
        d.start()
    for d in copies:
        d.wait()


def body(errors, saved_codes, active_mask, decoder):
    n = len(NAMES)
    results_shape = (
        jax.ShapeDtypeStruct((1, 256, 512), jnp.bfloat16),
        jax.ShapeDtypeStruct((1, 2, 512, 2048), jnp.bfloat16),
    )
    results = pl.pallas_call(
        kernel,
        out_shape=results_shape,
        in_specs=[pl.BlockSpec(memory_space=pltpu.HBM)] * 4,
        out_specs=(pl.BlockSpec(memory_space=pltpu.VMEM),) * 2,
        scratch_shapes=[
            pltpu.VMEM((2, 1024, 2048), jnp.bfloat16),
            pltpu.VMEM((1024, 512), jnp.bfloat16),
            pltpu.VMEM((512, 1024), jnp.bfloat16),
            pltpu.VMEM((2, 512, 2048), jnp.bfloat16),
            pltpu.VMEM((256, 512), jnp.int32),
            pltpu.VMEM((4, 256, 512), jnp.float32),
            pltpu.VMEM((12, 64, 512), jnp.int16),
            pltpu.VMEM((12, 1, 512), jnp.float32),
            pltpu.VMEM((12, 64, 512), jnp.int16),
            pltpu.VMEM((12, 1, 512), jnp.float32),
            pltpu.SemaphoreType.DMA((4,)),
            pltpu.SemaphoreType.DMA((n,)),
            pltpu.SemaphoreType.DMA((n,)),
        ],
        compiler_params=pltpu.CompilerParams(
            collective_id=0, has_side_effects=True, vmem_limit_bytes=48 * 1024 * 1024
        ),
    )(*(pltpu.with_memory_space_constraint(a, pltpu.HBM) for a in (errors, saved_codes, active_mask, decoder)))
    return pl.pallas_call(
        write_out,
        out_shape=results_shape,
        in_specs=[pl.BlockSpec(memory_space=pltpu.VMEM)] * 2,
        out_specs=(pl.BlockSpec(memory_space=pl.ANY),) * 2,
        scratch_shapes=[pltpu.SemaphoreType.DMA((9,))],
        compiler_params=pltpu.CompilerParams(vmem_limit_bytes=8 * 1024 * 1024),
    )(*results)


def solution(mesh):
    in_specs = (
        P("tgt", "feat", "src"),
        P("src", None, "feat"),
        P("src", "tgt", "feat"),
        P("src", "tgt", "feat", None),
    )
    out_specs = (P("src", "tgt", "feat"), P("src", "tgt", "feat", None))
    return jax.shard_map(body, mesh=mesh, in_specs=in_specs, out_specs=out_specs, check_vma=False)
```

```python
import jax
import jax.numpy as jnp
from jax import lax
from jax.experimental import pallas as pl
from jax.experimental.pallas import tpu as pltpu
from jax.sharding import PartitionSpec as P

MESH = pl.DeviceIdType.MESH

NAMES = (
    ["Z0", "Z1"]
    + [a + b for a in "XY" for b in ("fA", "bA", "rfA", "rbA", "Vf", "Vb", "Vo")]
    + [a + b + i for a in "PQ" for b in ("f", "b", "rf", "rb") for i in "AZ123"]
    + ["D00", "D10", "D11", "D12"]
    + [a + str(i) for a in ("D01", "D02", "D03", "D13") for i in range(4)]
    + [a + str(i) for a in "RS" for i in range(12)]
)
IDS = {name: i for i, name in enumerate(NAMES)}


def kernel(err, codes, mask, dec_hbm, cg, dw, E, codes_v, codes_t, dec, mask_v, part, qout, sout, qin, sin, local, ssem, rsem):
    s, t, f = lax.axis_index("src"), lax.axis_index("tgt"), lax.axis_index("feat")
    x, zl = s // 2, s % 2
    y, c = f // 2, f % 2
    step = 1 - 2 * zl
    xf, xb, xo = (x + step + 4) % 4, (x - step + 4) % 4, (x + 2) % 4
    yf, yb, yo = (y + step + 4) % 4, (y - step + 4) % 4, (y + 2) % 4
    X_F, X_B = {"src": xf * 2 + zl}, {"src": xb * 2 + zl}
    Y_F, Y_B = {"feat": yf * 2 + c}, {"feat": yb * 2 + c}
    Z_P, C_P = {"src": x * 2 + 1 - zl}, {"feat": y * 2 + 1 - c}
    T_UP, T_DN = {"tgt": (t + 1) % 4}, {"tgt": (t + 3) % 4}

    oz = 1 - zl
    ys, xs = (y, yb, yf, yo), (x, xb, xf, xo)

    def rows(yy, cc, half=None):
        if half is None:
            return pl.ds(pl.multiple_of((2 * yy + cc) * 128, 128), 128)
        return pl.ds(pl.multiple_of((2 * yy + cc) * 128 + half * 64, 64), 64)

    def item(layer, xx, z, yy, half=None):
        return E.at[layer, rows(yy, c, half), pl.ds(pl.multiple_of((2 * xx + z) * 256, 256), 256)]

    def pair(layer, xx, yy, half=None):
        return E.at[layer, rows(yy, c, half), pl.ds(pl.multiple_of(xx * 512, 512), 512)]

    def line(layer, yy, cc):
        return E.at[layer, rows(yy, cc), :]

    sent = []

    def copy(name, src, dst, dev):
        i = IDS[name]
        return pltpu.make_async_remote_copy(
            src_ref=src, dst_ref=dst, send_sem=ssem.at[i], recv_sem=rsem.at[i],
            device_id=dev, device_id_type=MESH,
        )

    def send(name, src, dev, dst=None):
        d = copy(name, src, src if dst is None else dst, dev)
        d.start()
        sent.append(d)

    def got(name, ref):
        copy(name, ref, ref, C_P).wait_recv()

    own_cols = pl.ds(pl.multiple_of(s * 256, 256), 256)
    own = E.at[:, rows(y, c), own_cols]
    load_err = pltpu.make_async_copy(err, own, local.at[0])
    load_codes = pltpu.make_async_copy(codes.at[0], codes_v, local.at[1])
    load_dec = pltpu.make_async_copy(dec_hbm.at[0], dec, local.at[2])
    load_mask = pltpu.make_async_copy(mask.at[0], mask_v, local.at[3])
    load_err.start()
    load_codes.start()
    load_dec.start()
    load_mask.start()

    barrier = pltpu.get_barrier_semaphore()
    for dev in (X_F, X_B, Y_F, Y_B, Z_P, C_P, T_UP, T_DN):
        pl.semaphore_signal(barrier, inc=1, device_id=dev, device_id_type=MESH)
    pl.semaphore_wait(barrier, 8)
    load_err.wait()

    def first(layer, kind, where):
        ax, (fw, bw) = ("X", (X_F, X_B)) if layer == 0 else ("Y", (Y_F, Y_B))
        send(ax + "f" + kind, where, fw)
        send(ax + "b" + kind, where, bw)

    def second(layer, piece, where):
        ax, (fw, bw) = ("P", (Y_F, Y_B)) if layer == 0 else ("Q", (X_F, X_B))
        send(ax + "f" + piece, where, fw)
        send(ax + "b" + piece, where, bw)

    own0, own1 = item(0, x, zl, y), item(1, x, zl, y)
    send("Z0", own0, Z_P)
    send("Z1", own1, Z_P)
    first(0, "A", own0)
    first(1, "A", own1)
    second(1, "A", own1)
    second(0, "A", own0)

    load_codes.wait()
    for i in range(4):
        codes_t[i * 128 : (i + 1) * 128, :] = codes_v[:, i * 128 : (i + 1) * 128].T

    def first_relay(layer, way):
        if layer == 0:
            near, dev, half = (xb, X_F, 0) if way == "f" else (xf, X_B, 1)
            got("X" + way + "A", item(0, near, zl, y))
            send("Xr" + way + "A", item(0, near, zl, y, half), dev)
        else:
            near, dev, half = (yb, Y_F, 0) if way == "f" else (yf, Y_B, 1)
            got("Y" + way + "A", item(1, x, zl, near))
            send("Yr" + way + "A", item(1, x, zl, near, half), dev)

    def first_rest(layer):
        if layer == 0:
            got("XrfA", item(0, xo, zl, y, 0))
            got("XrbA", item(0, xo, zl, y, 1))
        else:
            got("YrfA", item(1, x, zl, yo, 0))
            got("YrbA", item(1, x, zl, yo, 1))

    def across(layer, way):
        if layer == 0:
            send("XV" + way, item(0, {"f": xb, "b": xf, "o": xo}[way], zl, y), Z_P)
        else:
            send("YV" + way, item(1, x, zl, {"f": yb, "b": yf, "o": yo}[way]), Z_P)

    def crossed(layer, way):
        if layer == 0:
            got("XV" + way, item(0, {"f": xf, "b": xb, "o": xo}[way], oz, y))
        else:
            got("YV" + way, item(1, x, oz, {"f": yf, "b": yb, "o": yo}[way]))

    def piece_at(layer, piece, near, half=None):
        if piece in "AZ":
            z = zl if piece == "A" else oz
            return item(0, x, z, near, half) if layer == 0 else item(1, near, z, y, half)
        i = int(piece)
        return pair(0, xs[i], near, half) if layer == 0 else pair(1, near, ys[i], half)

    def second_relay(layer, piece):
        ax, (fw, bw), (nb, nf) = ("P", (Y_F, Y_B), (yb, yf)) if layer == 0 else ("Q", (X_F, X_B), (xb, xf))
        got(ax + "f" + piece, piece_at(layer, piece, nb))
        send(ax + "rf" + piece, piece_at(layer, piece, nb, 0), fw)
        got(ax + "b" + piece, piece_at(layer, piece, nf))
        send(ax + "rb" + piece, piece_at(layer, piece, nf, 1), bw)

    def second_rest(layer, piece):
        ax, far = ("P", yo) if layer == 0 else ("Q", xo)
        got(ax + "rf" + piece, piece_at(layer, piece, far, 0))
        got(ax + "rb" + piece, piece_at(layer, piece, far, 1))

    got("Z0", item(0, x, oz, y))
    second(0, "Z", item(0, x, oz, y))
    first_relay(0, "f")
    across(0, "f")
    first_relay(0, "b")
    across(0, "b")
    first_relay(1, "f")
    across(1, "f")
    first_relay(1, "b")
    got("Z1", item(1, x, oz, y))
    second(1, "Z", item(1, x, oz, y))
    second_relay(1, "A")
    crossed(0, "f")
    second(0, "2", pair(0, xf, y))
    first_rest(0)
    across(0, "o")
    across(1, "b")
    second_relay(1, "Z")
    crossed(0, "b")
    second(0, "1", pair(0, xb, y))
    first_rest(1)
    across(1, "o")
    crossed(1, "f")
    second(1, "2", pair(1, x, yf))
    crossed(0, "o")
    second(0, "3", pair(0, xo, y))
    send("D00", line(0, y, c), C_P)
    crossed(1, "b")
    second(1, "1", pair(1, x, yb))
    second_rest(1, "A")
    second_rest(1, "Z")
    send("D10", line(1, y, c), C_P)
    crossed(1, "o")

    live0, live1 = 2 * t >= s, 2 * t + 1 >= s

    def code_part(layer, k, opening):
        block = pl.ds(pl.multiple_of(ys[k] * 256, 256), 256)
        def product():
            return lax.dot_general(
                E[layer, block, :], dec[layer], (((1,), (1,)), ((), ())),
                preferred_element_type=jnp.float32,
            )

        live = (live0, live1)[layer]

        if opening:

            @pl.when(live)
            def _():
                part[k] = product()

            @pl.when(jnp.logical_not(live))
            def _():
                part[k] = jnp.zeros((256, 512), jnp.float32)
        else:

            @pl.when(live)
            def _():
                part[k] += product()

    def push(i, value, dev):
        most = jnp.max(jnp.abs(value), axis=0, keepdims=True)
        fits = most > 1e-33
        inverse = jnp.where(fits, 32767.0 / jnp.where(fits, most, 1.0), 0.0)
        qout[i] = jnp.round(value * inverse).astype(jnp.int32).astype(jnp.int16)
        sout[i] = most * (1.0 / 32767.0)
        copy("S%d" % i, sout.at[i], sin.at[i], dev).start()
        copy("R%d" % i, qout.at[i], qin.at[i], dev).start()

    def pull(i):
        got("S%d" % i, sin.at[i])
        got("R%d" % i, qin.at[i])
        return qin[i].astype(jnp.int32).astype(jnp.float32) * sin[i]

    los = (slice(0, 64), slice(64, 128))
    his = (slice(128, 192), slice(192, 256))

    def reduce_start(k):
        d = (t - ys[k] + 4) % 4

        @pl.when(d == 2)
        def _():
            for h in range(2):
                push(0 + h, part[k, los[h]], T_DN)
                push(2 + h, part[k, his[h]], T_UP)

        @pl.when(d == 1)
        def _():
            for h in range(2):
                push(4 + h, part[k, his[h]], T_DN)

        @pl.when(d == 3)
        def _():
            for h in range(2):
                push(8 + h, part[k, los[h]], T_UP)

    def reduce_next(k, halves=(0, 1)):
        d = (t - ys[k] + 4) % 4

        @pl.when(d == 1)
        def _():
            for h in halves:
                push(6 + h, part[k, los[h]] + pull(0 + h), T_DN)

        @pl.when(d == 3)
        def _():
            for h in halves:
                push(10 + h, part[k, his[h]] + pull(2 + h), T_UP)

    def chip_rows(i):
        send("D02%d" % i, pair(0, xs[i], yf), C_P)
        send("D01%d" % i, pair(0, xs[i], yb), C_P)

    def partner_pairs(layer, k, order):
        for i in order:
            got("D%d%d%d" % (layer, k, i), E.at[layer, rows(ys[k], 1 - c), pl.ds(pl.multiple_of(xs[i] * 512, 512), 512)])

    load_dec.wait()
    got("D00", line(0, y, 1 - c))
    code_part(0, 0, True)
    second_relay(0, "A")
    second_relay(0, "Z")
    chip_rows(0)
    second_relay(1, "2")
    got("D10", line(1, y, 1 - c))
    code_part(1, 0, False)
    reduce_start(0)
    second_relay(1, "1")
    second(1, "3", pair(1, x, yo))
    second_relay(0, "2")
    chip_rows(2)
    second_relay(0, "1")
    chip_rows(1)
    second_rest(1, "2")
    send("D12", line(1, yf, c), C_P)
    second_rest(1, "1")
    send("D11", line(1, yb, c), C_P)
    got("D12", line(1, yf, 1 - c))
    code_part(1, 2, True)
    second_relay(0, "3")
    chip_rows(3)
    got("D11", line(1, yb, 1 - c))
    code_part(1, 1, True)
    second_relay(1, "3")
    partner_pairs(0, 2, (0, 2, 1, 3))
    code_part(0, 2, False)
    reduce_start(2)
    partner_pairs(0, 1, (0, 2, 1, 3))
    code_part(0, 1, False)
    reduce_start(1)
    second_rest(0, "A")
    second_rest(0, "Z")
    send("D030", pair(0, x, yo), C_P)
    send("D130", pair(1, x, yo), C_P)
    send("D131", pair(1, xb, yo), C_P)
    send("D132", pair(1, xf, yo), C_P)
    for i, piece in ((2, "2"), (1, "1")):
        second_rest(0, piece)
        send("D03%d" % i, pair(0, xs[i], yo), C_P)
    second_rest(1, "3")
    send("D133", pair(1, xo, yo), C_P)
    second_rest(0, "3")
    send("D033", pair(0, xo, yo), C_P)
    partner_pairs(1, 3, range(4))
    code_part(1, 3, True)
    partner_pairs(0, 3, (0, 2, 1, 3))
    code_part(0, 3, False)
    reduce_start(3)
    reduce_next(2)
    reduce_next(1)
    reduce_next(0)

    def tile_grads(layer, live, start, stop):
        @pl.when(live)
        def _():
            def one(i, carry):
                cols = pl.ds(pl.multiple_of(i * 256, 256), 256)
                dw[0, layer, :, cols] = jnp.dot(
                    codes_t[...], E[layer, :, cols], preferred_element_type=jnp.float32
                ).astype(jnp.bfloat16)
                return carry

            lax.fori_loop(start, stop, one, 0)

        @pl.when(jnp.logical_not(live))
        def _():
            dw[0, layer, :, start * 256 : stop * 256] = jnp.zeros((512, (stop - start) * 256), jnp.bfloat16)

    tile_grads(0, live0, 0, 4)
    tile_grads(0, live0, 4, 8)
    tile_grads(1, live1, 0, 3)
    reduce_next(3, (0,))
    reduce_next(3, (1,))
    for k in range(4):

        @pl.when(ys[k] == t)
        def _():
            for h in range(2):
                part[k, los[h]] += pull(8 + h)
                part[k, his[h]] += pull(4 + h)

    tile_grads(1, live1, 3, 8)

    load_mask.wait()
    for k in range(4):

        @pl.when(ys[k] == t)
        def _():
            for h in range(2):
                low = part[k, los[h]] + pull(6 + h)
                cg[0, los[h]] = (low * mask_v[los[h]].astype(jnp.float32)).astype(jnp.bfloat16)
                high = part[k, his[h]] + pull(10 + h)
                cg[0, his[h]] = (high * mask_v[his[h]].astype(jnp.float32)).astype(jnp.bfloat16)

    for d in sent:
        d.wait_send()
    for i in range(12):
        copy("S%d" % i, sout.at[i], sin.at[i], C_P).wait_send()
        copy("R%d" % i, qout.at[i], qin.at[i], C_P).wait_send()


def write_out(cg_v, dw_v, cg, dw, sems):
    copies = [pltpu.make_async_copy(cg_v, cg, sems.at[8])]
    for i in range(8):
        at = (0, i // 4, pl.ds(i % 4 * 128, 128))
        copies.append(pltpu.make_async_copy(dw_v.at[at], dw.at[at], sems.at[i]))
    for d in copies:
        d.start()
    for d in copies:
        d.wait()


def body(errors, saved_codes, active_mask, decoder):
    n = len(NAMES)
    results_shape = (
        jax.ShapeDtypeStruct((1, 256, 512), jnp.bfloat16),
        jax.ShapeDtypeStruct((1, 2, 512, 2048), jnp.bfloat16),
    )
    results = pl.pallas_call(
        kernel,
        out_shape=results_shape,
        in_specs=[pl.BlockSpec(memory_space=pltpu.HBM)] * 4,
        out_specs=(pl.BlockSpec(memory_space=pltpu.VMEM),) * 2,
        scratch_shapes=[
            pltpu.VMEM((2, 1024, 2048), jnp.bfloat16),
            pltpu.VMEM((1024, 512), jnp.bfloat16),
            pltpu.VMEM((512, 1024), jnp.bfloat16),
            pltpu.VMEM((2, 512, 2048), jnp.bfloat16),
            pltpu.VMEM((256, 512), jnp.int32),
            pltpu.VMEM((4, 256, 512), jnp.float32),
            pltpu.VMEM((12, 64, 512), jnp.int16),
            pltpu.VMEM((12, 1, 512), jnp.float32),
            pltpu.VMEM((12, 64, 512), jnp.int16),
            pltpu.VMEM((12, 1, 512), jnp.float32),
            pltpu.SemaphoreType.DMA((4,)),
            pltpu.SemaphoreType.DMA((n,)),
            pltpu.SemaphoreType.DMA((n,)),
        ],
        compiler_params=pltpu.CompilerParams(
            collective_id=0, has_side_effects=True, vmem_limit_bytes=48 * 1024 * 1024
        ),
    )(*(pltpu.with_memory_space_constraint(a, pltpu.HBM) for a in (errors, saved_codes, active_mask, decoder)))
    return pl.pallas_call(
        write_out,
        out_shape=results_shape,
        in_specs=[pl.BlockSpec(memory_space=pltpu.VMEM)] * 2,
        out_specs=(pl.BlockSpec(memory_space=pl.ANY),) * 2,
        scratch_shapes=[pltpu.SemaphoreType.DMA((9,))],
        compiler_params=pltpu.CompilerParams(vmem_limit_bytes=8 * 1024 * 1024),
    )(*results)


def solution(mesh):
    in_specs = (
        P("tgt", "feat", "src"),
        P("src", None, "feat"),
        P("src", "tgt", "feat"),
        P("src", "tgt", "feat", None),
    )
    out_specs = (P("src", "tgt", "feat"), P("src", "tgt", "feat", None))
    return jax.shard_map(body, mesh=mesh, in_specs=in_specs, out_specs=out_specs, check_vma=False)
```
